512 devices in a mesh: ctx: 64 (over z_hi, y, x, core), tp: 8 (over z_lo).
Axes of the slice: x: 4, y: 4, z: 16 (z_hi: 2, z_lo: 8; z = z_hi * 8 + z_lo), core: 2. Of those that a mesh axis runs over, the one named last changes fastest.
Arguments:
- k_feature: bfloat16 [32, 524288], P('tp', 'ctx'), may hold values from -6 to 6
- v_feature: bfloat16 [32, 524288], P('tp', 'ctx'), may hold values from -6 to 6
- q_feature: bfloat16 [32, 524288], P('tp', 'ctx'), may hold values from -6 to 6
- spectrum: bfloat16 [2, 32, 1024, 1024], P(None, 'tp', 'ctx'), may hold values from -6 to 6
- skip_gain: float32 [32], P('tp'), may hold values from -1 to 1
- out_weight: bfloat16 [32, 64], replicated, may hold values from -1 to 1
Outputs:
- mixed: bfloat16 [64, 524288], P('tp', 'ctx')
The draws below stay inside these ranges and needn't reach their ends.
All inputs are finite; a program needn't handle non-finite values.
Results may differ from the reference program's by a relative error of at most 0.015.
Values may be sent and summed in bfloat16 or wider, within the bound.
A program may use at most 64 MiB of HBM per device.

```python
import math
import jax
import jax.numpy as jnp
from jax import lax

BLOCK = 1024
SEQ = 524288
CHANNELS = 32
OUTS = 64


def block_levels(own_key, dims, cuts, smallest, largest):
    gain = 1.0
    for position, shards_of in cuts:
        steps = jax.random.uniform(jax.random.fold_in(jax.random.fold_in(own_key, 6), position), (shards_of,), jnp.float32, smallest / len(cuts), largest / len(cuts))
        gain = gain * jnp.repeat(jnp.exp(steps), dims[position] // shards_of).reshape((-1,) + (1,) * (len(dims) - 1 - position))
    return gain


def bell_draw(key, shape, width, most, cuts=(), kind=jnp.bfloat16):
    values = width * jax.random.normal(key, shape, jnp.float32)
    if cuts:
        values = values * block_levels(key, shape, cuts, -0.22, 0.18)
    return jnp.clip(values, -most, most).astype(kind)


def setup_inputs(seed: int = 0) -> dict:
    streams_of = jax.random.split(jax.random.key(seed), 7)
    k_feature = bell_draw(streams_of[0], (CHANNELS, SEQ), 1.0, 6.0, ((0, 8), (1, 64)))
    v_feature = bell_draw(streams_of[1], (CHANNELS, SEQ), 1.0, 6.0, ((0, 8), (1, 64)))
    q_feature = bell_draw(streams_of[2], (CHANNELS, SEQ), 1.0, 6.0, ((0, 8), (1, 64)))
    spectrum = bell_draw(streams_of[3], (2, CHANNELS, BLOCK, BLOCK), 1.0, 6.0, ((1, 8), (2, 64)))
    skip_gain = jnp.clip(jax.random.uniform(streams_of[4], (CHANNELS,), jnp.float32, -1.0, 1.0) * block_levels(streams_of[4], (CHANNELS,), ((0, 8),), -0.4, 0.0), -1.0, 1.0)
    out_weight = bell_draw(streams_of[5], (CHANNELS, OUTS), CHANNELS ** -0.5, 1.0)
    return dict(k_feature=k_feature, v_feature=v_feature, q_feature=q_feature, spectrum=spectrum, skip_gain=skip_gain, out_weight=out_weight)


def fourier_tables(length_all):
    positions = jnp.arange(length_all, dtype=jnp.int32)
    phase_index = (positions[:, None] * positions[None, :]) % length_all
    angles = phase_index.astype(jnp.float32) * (2.0 * math.pi / length_all)
    return jnp.cos(angles).astype(jnp.bfloat16), jnp.sin(angles).astype(jnp.bfloat16)


def twist_tables(left_index, right_index, length_all):
    phase_index = (left_index[:, None] * right_index[None, :]) % length_all
    angles = phase_index.astype(jnp.float32) * (2.0 * math.pi / length_all)
    return jnp.cos(angles), jnp.sin(angles)


def reference(k_feature, v_feature, q_feature, spectrum, skip_gain, out_weight):
    length_all = BLOCK * BLOCK
    product = (k_feature.astype(jnp.float32) * v_feature.astype(jnp.float32)).astype(jnp.bfloat16)
    cosine_full, sine_full = fourier_tables(BLOCK)
    cosine_half = cosine_full[: BLOCK // 2]
    sine_half = sine_full[: BLOCK // 2]
    positions = jnp.arange(BLOCK, dtype=jnp.int32)
    twist_cosine, twist_sine = twist_tables(positions, positions, length_all)

    def convolve(members):
        signal, response = members
        grid_rows = signal.reshape(BLOCK // 2, BLOCK)
        first_real = jnp.dot(cosine_half.T, grid_rows, preferred_element_type=jnp.float32)
        first_imag = -jnp.dot(sine_half.T, grid_rows, preferred_element_type=jnp.float32)
        spread_real = (first_real * twist_cosine + first_imag * twist_sine).astype(jnp.bfloat16)
        spread_imag = (first_imag * twist_cosine - first_real * twist_sine).astype(jnp.bfloat16)
        freq_real = jnp.dot(spread_real, cosine_full, preferred_element_type=jnp.float32) + jnp.dot(spread_imag, sine_full, preferred_element_type=jnp.float32)
        freq_imag = jnp.dot(spread_imag, cosine_full, preferred_element_type=jnp.float32) - jnp.dot(spread_real, sine_full, preferred_element_type=jnp.float32)
        resp_real = response[0].astype(jnp.float32)
        resp_imag = response[1].astype(jnp.float32)
        shaped_real = (freq_real * resp_real - freq_imag * resp_imag).astype(jnp.bfloat16)
        shaped_imag = (freq_real * resp_imag + freq_imag * resp_real).astype(jnp.bfloat16)
        inner_real = jnp.dot(shaped_real, cosine_full, preferred_element_type=jnp.float32) - jnp.dot(shaped_imag, sine_full, preferred_element_type=jnp.float32)
        inner_imag = jnp.dot(shaped_imag, cosine_full, preferred_element_type=jnp.float32) + jnp.dot(shaped_real, sine_full, preferred_element_type=jnp.float32)
        back_real = (inner_real * twist_cosine - inner_imag * twist_sine).astype(jnp.bfloat16)
        back_imag = (inner_imag * twist_cosine + inner_real * twist_sine).astype(jnp.bfloat16)
        summed = jnp.dot(cosine_half, back_real, preferred_element_type=jnp.float32) - jnp.dot(sine_half, back_imag, preferred_element_type=jnp.float32)
        return (summed * (1.0 / length_all)).astype(jnp.bfloat16).reshape(SEQ)

    convolved = lax.map(convolve, (product, jnp.moveaxis(spectrum, 1, 0)))
    gated_rows = (q_feature.astype(jnp.float32) * (convolved.astype(jnp.float32) + skip_gain[:, None] * product.astype(jnp.float32))).astype(jnp.bfloat16)
    return jnp.dot(out_weight.T, gated_rows, preferred_element_type=jnp.float32).astype(jnp.bfloat16)
```

```python
import math

import jax
import jax.numpy as jnp
from jax import lax
from jax.sharding import PartitionSpec as P


def fourier_tables(length_all):
    split = 1 << (int(math.log2(length_all)) // 2)
    rows_hi = length_all // split
    scale = 2.0 * math.pi / length_all
    columns = jnp.arange(length_all, dtype=jnp.int32)
    low = jnp.arange(split, dtype=jnp.int32)
    high = jnp.arange(rows_hi, dtype=jnp.int32)
    angle_low = (low[:, None] * columns[None, :] % length_all).astype(jnp.float32) * scale
    angle_high = (split * high[:, None] * columns[None, :] % length_all).astype(jnp.float32) * scale
    cos_low, sin_low = jnp.cos(angle_low)[None], jnp.sin(angle_low)[None]
    cos_high, sin_high = jnp.cos(angle_high)[:, None], jnp.sin(angle_high)[:, None]
    cosine = (cos_high * cos_low - sin_high * sin_low).reshape(length_all, length_all)
    sine = (sin_high * cos_low + cos_high * sin_low).reshape(length_all, length_all)
    return lax.optimization_barrier((cosine.astype(jnp.bfloat16), sine.astype(jnp.bfloat16)))


def twist_tables(left_index, right_index, length_all):
    phase_index = left_index[:, None] * right_index[None, :] % length_all
    angles = phase_index.astype(jnp.float32) * (2.0 * math.pi / length_all)
    return (jnp.cos(angles), jnp.sin(angles))


def contract(form, left, right):
    return jnp.einsum(form, left, right, preferred_element_type=jnp.float32)


def local(k_feature, v_feature, q_feature, spectrum, skip_gain, out_weight):
    channels, tokens = k_feature.shape
    block_order = spectrum.shape[3]
    length_all = block_order * block_order
    ctx_count = lax.axis_size("ctx")
    tp_count = lax.axis_size("tp")
    slab_width = block_order // ctx_count
    rows_here = tokens // block_order
    ctx_index = lax.axis_index("ctx")
    product = (k_feature.astype(jnp.float32) * v_feature.astype(jnp.float32)).astype(jnp.bfloat16)
    cosine_full, sine_full = fourier_tables(block_order)
    cosine_half = cosine_full[: block_order // 2]
    sine_half = sine_full[: block_order // 2]
    positions = jnp.arange(block_order, dtype=jnp.int32)
    local_ticks = ctx_index * slab_width + jnp.arange(slab_width, dtype=jnp.int32)
    grid_rows = lax.all_to_all(
        product.reshape(channels, rows_here, block_order),
        "ctx",
        split_axis=2,
        concat_axis=1,
        tiled=True,
    )
    first_real = contract("cij,ia->caj", grid_rows, cosine_half)
    first_imag = -contract("cij,ia->caj", grid_rows, sine_half)
    twist_cosine, twist_sine = twist_tables(positions, local_ticks, length_all)
    spread_real = (first_real * twist_cosine + first_imag * twist_sine).astype(jnp.bfloat16)
    spread_imag = (first_imag * twist_cosine - first_real * twist_sine).astype(jnp.bfloat16)
    block_real, block_imag = (
        lax.all_to_all(spread_real, "ctx", split_axis=1, concat_axis=2, tiled=True),
        lax.all_to_all(spread_imag, "ctx", split_axis=1, concat_axis=2, tiled=True),
    )
    freq_real = contract("caj,jb->cab", block_real, cosine_full) + contract(
        "caj,jb->cab", block_imag, sine_full
    )
    freq_imag = contract("caj,jb->cab", block_imag, cosine_full) - contract(
        "caj,jb->cab", block_real, sine_full
    )
    resp_real = spectrum[0].astype(jnp.float32)
    resp_imag = spectrum[1].astype(jnp.float32)
    shaped_real = (freq_real * resp_real - freq_imag * resp_imag).astype(jnp.bfloat16)
    shaped_imag = (freq_real * resp_imag + freq_imag * resp_real).astype(jnp.bfloat16)
    inner_real = contract("cab,bj->caj", shaped_real, cosine_full) - contract(
        "cab,bj->caj", shaped_imag, sine_full
    )
    inner_imag = contract("cab,bj->caj", shaped_imag, cosine_full) + contract(
        "cab,bj->caj", shaped_real, sine_full
    )
    twist_cosine, twist_sine = twist_tables(local_ticks, positions, length_all)
    back_real = (inner_real * twist_cosine - inner_imag * twist_sine).astype(jnp.bfloat16)
    back_imag = (inner_imag * twist_cosine + inner_real * twist_sine).astype(jnp.bfloat16)
    summed = contract(
        "ia,caj->cij",
        cosine_half,
        lax.all_to_all(back_real, "ctx", split_axis=2, concat_axis=1, tiled=True),
    ) - contract(
        "ia,caj->cij",
        sine_half,
        lax.all_to_all(back_imag, "ctx", split_axis=2, concat_axis=1, tiled=True),
    )
    spatial = (summed * (1.0 / length_all)).astype(jnp.bfloat16)
    convolved = lax.all_to_all(spatial, "ctx", split_axis=1, concat_axis=2, tiled=True).reshape(
        channels, tokens
    )
    gated_rows = (
        q_feature.astype(jnp.float32)
        * (convolved.astype(jnp.float32) + skip_gain[:, None] * product.astype(jnp.float32))
    ).astype(jnp.bfloat16)
    gated_all = lax.all_gather(gated_rows, "tp", axis=0, tiled=True)
    outs_here = out_weight.shape[1] // tp_count
    tp_index = lax.axis_index("tp")
    my_weight = lax.dynamic_slice_in_dim(out_weight, tp_index * outs_here, outs_here, 1)
    return jnp.dot(my_weight.T, gated_all, preferred_element_type=jnp.float32).astype(jnp.bfloat16)


def solution(mesh):
    placed = (
        P("tp", "ctx"),
        P("tp", "ctx"),
        P("tp", "ctx"),
        P(None, "tp", "ctx", None),
        P("tp"),
        P(),
    )
    return jax.shard_map(
        local, mesh=mesh, in_specs=placed, out_specs=P("tp", "ctx"), check_vma=False
    )
```

```python
import functools
import math

import jax
import jax.numpy as jnp
from jax import lax
from jax.experimental import pallas as pl
from jax.experimental.pallas import tpu as pltpu
from jax.sharding import PartitionSpec as P

MESH = pl.DeviceIdType.MESH


def _exchange_kernel(axis, gather, x_ref, y_ref, land, send_sem, recv_sem, local_sem):
    count = land.shape[0]
    me = lax.axis_index(axis)
    barrier = pltpu.get_barrier_semaphore()

    def greet(step, carry):
        peer = lax.rem(me + step, count)
        pl.semaphore_signal(barrier, 1, device_id={axis: peer}, device_id_type=MESH)
        return carry

    lax.fori_loop(1, count, greet, 0)
    pl.semaphore_wait(barrier, count - 1)

    def piece(peer):
        return x_ref if gather else x_ref.at[peer]

    def outgoing(peer):
        return pltpu.make_async_remote_copy(
            src_ref=piece(peer), dst_ref=land.at[me], send_sem=send_sem.at[peer],
            recv_sem=recv_sem.at[me], device_id={axis: peer}, device_id_type=MESH)

    def incoming(source):
        return pltpu.make_async_remote_copy(
            src_ref=piece(source), dst_ref=land.at[source], send_sem=send_sem.at[source],
            recv_sem=recv_sem.at[source], device_id={axis: source}, device_id_type=MESH)

    def send(step, carry):
        outgoing(lax.rem(me + step, count)).start()
        return carry

    lax.fori_loop(1, count, send, 0)
    local = pltpu.make_async_copy(piece(me), land.at[me], local_sem)
    local.start()

    def finish(step, carry):
        outgoing(lax.rem(me + step, count)).wait_send()
        incoming(lax.rem(me + count - step, count)).wait_recv()
        return carry

    lax.fori_loop(1, count, finish, 0)
    local.wait()
    y_ref[...] = land[...]


def exchange(x, axis, gather, collective):
    count = lax.axis_size(axis)
    chunk = x.shape if gather else x.shape[1:]
    full = (count,) + tuple(chunk)
    return pl.pallas_call(
        functools.partial(_exchange_kernel, axis, gather),
        out_shape=jax.ShapeDtypeStruct(full, x.dtype),
        in_specs=[pl.BlockSpec(memory_space=pltpu.VMEM)],
        out_specs=pl.BlockSpec(memory_space=pltpu.VMEM),
        scratch_shapes=[
            pltpu.VMEM(full, x.dtype),
            pltpu.SemaphoreType.DMA((count,)),
            pltpu.SemaphoreType.DMA((count,)),
            pltpu.SemaphoreType.DMA,
        ],
        compiler_params=pltpu.CompilerParams(collective_id=collective, has_side_effects=True),
    )(x)


def fourier_tables(length_all):
    split = 1 << (int(math.log2(length_all)) // 2)
    rows_hi = length_all // split
    scale = 2.0 * math.pi / length_all
    columns = jnp.arange(length_all, dtype=jnp.int32)
    low = jnp.arange(split, dtype=jnp.int32)
    high = jnp.arange(rows_hi, dtype=jnp.int32)
    angle_low = (low[:, None] * columns[None, :] % length_all).astype(jnp.float32) * scale
    angle_high = (split * high[:, None] * columns[None, :] % length_all).astype(jnp.float32) * scale
    cos_low, sin_low = jnp.cos(angle_low)[None], jnp.sin(angle_low)[None]
    cos_high, sin_high = jnp.cos(angle_high)[:, None], jnp.sin(angle_high)[:, None]
    cosine = (cos_high * cos_low - sin_high * sin_low).reshape(length_all, length_all)
    sine = (sin_high * cos_low + cos_high * sin_low).reshape(length_all, length_all)
    return lax.optimization_barrier((cosine.astype(jnp.bfloat16), sine.astype(jnp.bfloat16)))


def twist_tables(left_index, right_index, length_all):
    phase_index = left_index[:, None] * right_index[None, :] % length_all
    angles = phase_index.astype(jnp.float32) * (2.0 * math.pi / length_all)
    return (jnp.cos(angles), jnp.sin(angles))


def contract(form, left, right):
    return jnp.einsum(form, left, right, preferred_element_type=jnp.float32)


def local(k_feature, v_feature, q_feature, spectrum, skip_gain, out_weight):
    channels, tokens = k_feature.shape
    block_order = spectrum.shape[3]
    length_all = block_order * block_order
    ctx_count = lax.axis_size("ctx")
    tp_count = lax.axis_size("tp")
    slab_width = block_order // ctx_count
    rows_here = tokens // block_order
    half_rows = block_order // 2
    ctx_index = lax.axis_index("ctx")
    product = (k_feature.astype(jnp.float32) * v_feature.astype(jnp.float32)).astype(jnp.bfloat16)
    cosine_full, sine_full = fourier_tables(block_order)
    cosine_half = cosine_full[:half_rows]
    sine_half = sine_full[:half_rows]
    positions = jnp.arange(block_order, dtype=jnp.int32)
    local_ticks = ctx_index * slab_width + jnp.arange(slab_width, dtype=jnp.int32)

    outgoing = product.reshape(channels, rows_here, ctx_count, slab_width).transpose(2, 0, 1, 3)
    arrived = exchange(outgoing.reshape(ctx_count, channels, -1), "ctx", False, 0)
    grid_rows = (
        arrived.reshape(ctx_count, channels, rows_here, slab_width)
        .transpose(1, 0, 2, 3)
        .reshape(channels, half_rows, slab_width)
    )
    first_real = contract("cij,ia->caj", grid_rows, cosine_half)
    first_imag = -contract("cij,ia->caj", grid_rows, sine_half)
    twist_cosine, twist_sine = twist_tables(positions, local_ticks, length_all)
    spread_real = (first_real * twist_cosine + first_imag * twist_sine).astype(jnp.bfloat16)
    spread_imag = (first_imag * twist_cosine - first_real * twist_sine).astype(jnp.bfloat16)

    spread = jnp.stack([spread_real, spread_imag])
    outgoing = spread.reshape(2, channels, ctx_count, slab_width, slab_width).transpose(2, 0, 1, 3, 4)
    arrived = exchange(outgoing.reshape(ctx_count, -1, 128), "ctx", False, 1)
    block = (
        arrived.reshape(ctx_count, 2, channels, slab_width, slab_width)
        .transpose(1, 2, 3, 0, 4)
        .reshape(2, channels, slab_width, block_order)
    )
    block_real, block_imag = block[0], block[1]
    freq_real = contract("caj,jb->cab", block_real, cosine_full) + contract(
        "caj,jb->cab", block_imag, sine_full
    )
    freq_imag = contract("caj,jb->cab", block_imag, cosine_full) - contract(
        "caj,jb->cab", block_real, sine_full
    )
    resp_real = spectrum[0].astype(jnp.float32)
    resp_imag = spectrum[1].astype(jnp.float32)
    shaped_real = (freq_real * resp_real - freq_imag * resp_imag).astype(jnp.bfloat16)
    shaped_imag = (freq_real * resp_imag + freq_imag * resp_real).astype(jnp.bfloat16)
    inner_real = contract("cab,bj->caj", shaped_real, cosine_full) - contract(
        "cab,bj->caj", shaped_imag, sine_full
    )
    inner_imag = contract("cab,bj->caj", shaped_imag, cosine_full) + contract(
        "cab,bj->caj", shaped_real, sine_full
    )
    twist_cosine, twist_sine = twist_tables(local_ticks, positions, length_all)
    back_real = (inner_real * twist_cosine - inner_imag * twist_sine).astype(jnp.bfloat16)
    back_imag = (inner_imag * twist_cosine + inner_real * twist_sine).astype(jnp.bfloat16)

    back = jnp.stack([back_real, back_imag])
    outgoing = back.reshape(2, channels, slab_width, ctx_count, slab_width).transpose(3, 0, 1, 2, 4)
    arrived = exchange(outgoing.reshape(ctx_count, -1, 128), "ctx", False, 2)
    columns = (
        arrived.reshape(ctx_count, 2, channels, slab_width, slab_width)
        .transpose(1, 2, 0, 3, 4)
        .reshape(2, channels, block_order, slab_width)
    )
    summed = contract("ia,caj->cij", cosine_half, columns[0]) - contract(
        "ia,caj->cij", sine_half, columns[1]
    )
    spatial = (summed * (1.0 / length_all)).astype(jnp.bfloat16)

    outgoing = spatial.reshape(channels, ctx_count, rows_here, slab_width).transpose(1, 0, 2, 3)
    arrived = exchange(outgoing.reshape(ctx_count, channels, -1), "ctx", False, 3)
    convolved = (
        arrived.reshape(ctx_count, channels, rows_here, slab_width)
        .transpose(1, 2, 0, 3)
        .reshape(channels, tokens)
    )
    gated_rows = (
        q_feature.astype(jnp.float32)
        * (convolved.astype(jnp.float32) + skip_gain[:, None] * product.astype(jnp.float32))
    ).astype(jnp.bfloat16)
    gated_all = exchange(gated_rows, "tp", True, 4).reshape(tp_count * channels, tokens)
    outs_here = out_weight.shape[1] // tp_count
    tp_index = lax.axis_index("tp")
    my_weight = lax.dynamic_slice_in_dim(out_weight, tp_index * outs_here, outs_here, 1)
    return jnp.dot(my_weight.T, gated_all, preferred_element_type=jnp.float32).astype(jnp.bfloat16)


def solution(mesh):
    placed = (
        P("tp", "ctx"),
        P("tp", "ctx"),
        P("tp", "ctx"),
        P(None, "tp", "ctx", None),
        P("tp"),
        P(),
    )
    return jax.shard_map(
        local, mesh=mesh, in_specs=placed, out_specs=P("tp", "ctx"), check_vma=False
    )
```

```python
import functools
import math

import jax
import jax.numpy as jnp
from jax import lax
from jax.experimental import pallas as pl
from jax.experimental.pallas import tpu as pltpu
from jax.sharding import PartitionSpec as P

MESH = pl.DeviceIdType.MESH


def _exchange_kernel(axis, gather, x_ref, y_ref, land, send_sem, recv_sem, local_sem):
    count = land.shape[0]
    me = lax.axis_index(axis)
    barrier = pltpu.get_barrier_semaphore()

    def greet(step, carry):
        peer = lax.rem(me + step, count)
        pl.semaphore_signal(barrier, 1, device_id={axis: peer}, device_id_type=MESH)
        return carry

    lax.fori_loop(1, count, greet, 0)
    pl.semaphore_wait(barrier, count - 1)

    def piece(peer):
        return x_ref if gather else x_ref.at[peer]

    def outgoing(peer):
        return pltpu.make_async_remote_copy(
            src_ref=piece(peer), dst_ref=land.at[me], send_sem=send_sem.at[peer],
            recv_sem=recv_sem.at[me], device_id={axis: peer}, device_id_type=MESH)

    def incoming(source):
        return pltpu.make_async_remote_copy(
            src_ref=piece(source), dst_ref=land.at[source], send_sem=send_sem.at[source],
            recv_sem=recv_sem.at[source], device_id={axis: source}, device_id_type=MESH)

    def send(step, carry):
        outgoing(lax.rem(me + step, count)).start()
        return carry

    lax.fori_loop(1, count, send, 0)
    local = pltpu.make_async_copy(piece(me), land.at[me], local_sem)
    local.start()

    def finish(step, carry):
        outgoing(lax.rem(me + step, count)).wait_send()
        incoming(lax.rem(me + count - step, count)).wait_recv()
        return carry

    lax.fori_loop(1, count, finish, 0)
    local.wait()
    y_ref[...] = land[...]


def exchange(x, axis, gather, collective):
    count = lax.axis_size(axis)
    chunk = x.shape if gather else x.shape[1:]
    full = (count,) + tuple(chunk)
    return pl.pallas_call(
        functools.partial(_exchange_kernel, axis, gather),
        out_shape=jax.ShapeDtypeStruct(full, x.dtype),
        in_specs=[pl.BlockSpec(memory_space=pltpu.VMEM)],
        out_specs=pl.BlockSpec(memory_space=pltpu.VMEM),
        scratch_shapes=[
            pltpu.VMEM(full, x.dtype),
            pltpu.SemaphoreType.DMA((count,)),
            pltpu.SemaphoreType.DMA((count,)),
            pltpu.SemaphoreType.DMA,
        ],
        compiler_params=pltpu.CompilerParams(collective_id=collective, has_side_effects=True),
    )(x)


def fourier_tables(length_all):
    split = 1 << (int(math.log2(length_all)) // 2)
    rows_hi = length_all // split
    scale = 2.0 * math.pi / length_all
    columns = jnp.arange(length_all, dtype=jnp.int32)
    low = jnp.arange(split, dtype=jnp.int32)
    high = jnp.arange(rows_hi, dtype=jnp.int32)
    angle_low = (low[:, None] * columns[None, :] % length_all).astype(jnp.float32) * scale
    angle_high = (split * high[:, None] * columns[None, :] % length_all).astype(jnp.float32) * scale
    cos_low, sin_low = jnp.cos(angle_low)[None], jnp.sin(angle_low)[None]
    cos_high, sin_high = jnp.cos(angle_high)[:, None], jnp.sin(angle_high)[:, None]
    cosine = (cos_high * cos_low - sin_high * sin_low).reshape(length_all, length_all)
    sine = (sin_high * cos_low + cos_high * sin_low).reshape(length_all, length_all)
    return lax.optimization_barrier((cosine.astype(jnp.bfloat16), sine.astype(jnp.bfloat16)))


def twist_tables(left_index, right_index, length_all):
    phase_index = left_index[:, None] * right_index[None, :] % length_all
    angles = phase_index.astype(jnp.float32) * (2.0 * math.pi / length_all)
    return (jnp.cos(angles), jnp.sin(angles))


def contract(form, left, right):
    return jnp.einsum(form, left, right, preferred_element_type=jnp.float32)


def local(k_feature, v_feature, q_feature, spectrum, skip_gain, out_weight):
    channels, tokens = k_feature.shape
    block_order = spectrum.shape[3]
    length_all = block_order * block_order
    ctx_count = lax.axis_size("ctx")
    tp_count = lax.axis_size("tp")
    slab = block_order // ctx_count
    rows_here = tokens // block_order
    half_rows = block_order // 2
    lanes = channels * slab
    ctx_index = lax.axis_index("ctx")
    product = (k_feature.astype(jnp.float32) * v_feature.astype(jnp.float32)).astype(jnp.bfloat16)
    cosine_full, sine_full = fourier_tables(block_order)
    both_full = jnp.stack([cosine_full, sine_full])
    both_half = both_full[:, :half_rows]
    positions = jnp.arange(block_order, dtype=jnp.int32)
    local_ticks = ctx_index * slab + jnp.arange(slab, dtype=jnp.int32)
    twist_cosine, twist_sine = twist_tables(positions, local_ticks, length_all)
    twist_cosine = jnp.tile(twist_cosine, (1, channels))
    twist_sine = jnp.tile(twist_sine, (1, channels))

    outgoing = product.reshape(channels, rows_here, ctx_count, slab).transpose(2, 1, 0, 3)
    arrived = exchange(outgoing.reshape(ctx_count, -1, 128), "ctx", False, 0)
    grid_rows = arrived.reshape(half_rows, lanes)
    first = contract("sia,ik->sak", both_half, grid_rows)
    spread = jnp.concatenate(
        [
            first[0] * twist_cosine - first[1] * twist_sine,
            -first[1] * twist_cosine - first[0] * twist_sine,
        ],
        axis=1,
    ).astype(jnp.bfloat16)

    arrived = exchange(spread.reshape(ctx_count, slab, 2 * lanes), "ctx", False, 1)
    block = (
        arrived.reshape(ctx_count, slab, 2, channels, slab)
        .transpose(0, 4, 2, 3, 1)
        .reshape(block_order, 2 * lanes)
    )
    freq = contract("sbj,jk->sbk", both_full, block)
    freq_real = freq[0, :, :lanes] + freq[1, :, lanes:]
    freq_imag = freq[0, :, lanes:] - freq[1, :, :lanes]
    response = spectrum.reshape(2, lanes, block_order).transpose(0, 2, 1).astype(jnp.float32)
    shaped = jnp.concatenate(
        [
            freq_real * response[0] - freq_imag * response[1],
            freq_real * response[1] + freq_imag * response[0],
        ],
        axis=1,
    ).astype(jnp.bfloat16)
    inner = contract("sjb,bk->sjk", both_full, shaped)
    inner_real = inner[0, :, :lanes] - inner[1, :, lanes:]
    inner_imag = inner[0, :, lanes:] + inner[1, :, :lanes]
    back = jnp.concatenate(
        [
            inner_real * twist_cosine - inner_imag * twist_sine,
            inner_imag * twist_cosine + inner_real * twist_sine,
        ],
        axis=1,
    ).astype(jnp.bfloat16)

    arrived = exchange(back.reshape(ctx_count, slab, 2 * lanes), "ctx", False, 2)
    columns = (
        arrived.reshape(ctx_count, slab, 2, channels, slab)
        .transpose(0, 4, 2, 3, 1)
        .reshape(block_order, 2 * lanes)
    )
    summed = contract("sia,ak->sik", both_half, columns)
    spatial = ((summed[0, :, :lanes] - summed[1, :, lanes:]) * (1.0 / length_all)).astype(
        jnp.bfloat16
    )

    arrived = exchange(spatial.reshape(ctx_count, -1, 128), "ctx", False, 3)
    convolved = (
        arrived.reshape(ctx_count, rows_here, channels, slab)
        .transpose(2, 1, 0, 3)
        .reshape(channels, tokens)
    )
    gated_rows = (
        q_feature.astype(jnp.float32)
        * (convolved.astype(jnp.float32) + skip_gain[:, None] * product.astype(jnp.float32))
    ).astype(jnp.bfloat16)
    gated_all = exchange(gated_rows, "tp", True, 4).reshape(tp_count * channels, tokens)
    outs_here = out_weight.shape[1] // tp_count
    tp_index = lax.axis_index("tp")
    my_weight = lax.dynamic_slice_in_dim(out_weight, tp_index * outs_here, outs_here, 1)
    return jnp.dot(my_weight.T, gated_all, preferred_element_type=jnp.float32).astype(jnp.bfloat16)


def solution(mesh):
    placed = (
        P("tp", "ctx"),
        P("tp", "ctx"),
        P("tp", "ctx"),
        P(None, "tp", "ctx", None),
        P("tp"),
        P(),
    )
    return jax.shard_map(
        local, mesh=mesh, in_specs=placed, out_specs=P("tp", "ctx"), check_vma=False
    )
```

```python
import functools
import math

import jax
import jax.numpy as jnp
from jax import lax
from jax.experimental import pallas as pl
from jax.experimental.pallas import tpu as pltpu
from jax.sharding import PartitionSpec as P

MESH = pl.DeviceIdType.MESH


def _exchange_kernel(axis, gather, x_ref, y_ref, land, send_sem, recv_sem, local_sem):
    count = land.shape[0]
    me = lax.axis_index(axis)
    barrier = pltpu.get_barrier_semaphore()

    def greet(step, carry):
        peer = lax.rem(me + step, count)
        pl.semaphore_signal(barrier, 1, device_id={axis: peer}, device_id_type=MESH)
        return carry

    lax.fori_loop(1, count, greet, 0)
    pl.semaphore_wait(barrier, count - 1)

    def piece(peer):
        return x_ref if gather else x_ref.at[peer]

    def outgoing(peer):
        return pltpu.make_async_remote_copy(
            src_ref=piece(peer), dst_ref=land.at[me], send_sem=send_sem.at[peer],
            recv_sem=recv_sem.at[me], device_id={axis: peer}, device_id_type=MESH)

    def incoming(source):
        return pltpu.make_async_remote_copy(
            src_ref=piece(source), dst_ref=land.at[source], send_sem=send_sem.at[source],
            recv_sem=recv_sem.at[source], device_id={axis: source}, device_id_type=MESH)

    def send(step, carry):
        outgoing(lax.rem(me + step, count)).start()
        return carry

    lax.fori_loop(1, count, send, 0)
    local = pltpu.make_async_copy(piece(me), land.at[me], local_sem)
    local.start()

    def finish(step, carry):
        outgoing(lax.rem(me + step, count)).wait_send()
        incoming(lax.rem(me + count - step, count)).wait_recv()
        return carry

    lax.fori_loop(1, count, finish, 0)
    local.wait()
    y_ref[...] = land[...]


def exchange(x, axis, gather, collective):
    count = lax.axis_size(axis)
    chunk = x.shape if gather else x.shape[1:]
    full = (count,) + tuple(chunk)
    return pl.pallas_call(
        functools.partial(_exchange_kernel, axis, gather),
        out_shape=jax.ShapeDtypeStruct(full, x.dtype),
        in_specs=[pl.BlockSpec(memory_space=pltpu.VMEM)],
        out_specs=pl.BlockSpec(memory_space=pltpu.VMEM),
        scratch_shapes=[
            pltpu.VMEM(full, x.dtype),
            pltpu.SemaphoreType.DMA((count,)),
            pltpu.SemaphoreType.DMA((count,)),
            pltpu.SemaphoreType.DMA,
        ],
        compiler_params=pltpu.CompilerParams(collective_id=collective, has_side_effects=True),
    )(x)


def _final_kernel(x_ref, y_ref, land, gathered, send_sem, recv_sem, fsend_sem, frecv_sem, local_sem):
    count = land.shape[0]
    groups = gathered.shape[0]
    me = lax.axis_index("ctx")
    mine = lax.axis_index("tp")
    barrier = pltpu.get_barrier_semaphore()

    def greet(step, carry):
        peer = lax.rem(me + step, count)
        pl.semaphore_signal(barrier, 1, device_id={"ctx": peer}, device_id_type=MESH)
        return carry

    def greet_tp(step, carry):
        peer = lax.rem(mine + step, groups)
        pl.semaphore_signal(barrier, 1, device_id={"tp": peer}, device_id_type=MESH)
        return carry

    lax.fori_loop(1, count, greet, 0)
    lax.fori_loop(1, groups, greet_tp, 0)
    pl.semaphore_wait(barrier, count + groups - 2)

    def outgoing(peer):
        return pltpu.make_async_remote_copy(
            src_ref=x_ref.at[peer], dst_ref=land.at[me], send_sem=send_sem.at[peer],
            recv_sem=recv_sem.at[me], device_id={"ctx": peer}, device_id_type=MESH)

    def incoming(source):
        return pltpu.make_async_remote_copy(
            src_ref=x_ref.at[source], dst_ref=land.at[source], send_sem=send_sem.at[source],
            recv_sem=recv_sem.at[source], device_id={"ctx": source}, device_id_type=MESH)

    def send(step, carry):
        outgoing(lax.rem(me + step, count)).start()
        return carry

    lax.fori_loop(1, count, send, 0)
    local = pltpu.make_async_copy(x_ref.at[me], land.at[me], local_sem.at[0])
    local.start()

    def finish(step, carry):
        outgoing(lax.rem(me + step, count)).wait_send()
        incoming(lax.rem(me + count - step, count)).wait_recv()
        return carry

    lax.fori_loop(1, count, finish, 0)
    local.wait()

    def forward(peer):
        return pltpu.make_async_remote_copy(
            src_ref=land, dst_ref=gathered.at[mine], send_sem=fsend_sem.at[peer],
            recv_sem=frecv_sem.at[mine], device_id={"tp": peer}, device_id_type=MESH)

    def collected(source):
        return pltpu.make_async_remote_copy(
            src_ref=land, dst_ref=gathered.at[source], send_sem=fsend_sem.at[source],
            recv_sem=frecv_sem.at[source], device_id={"tp": source}, device_id_type=MESH)

    def send_tp(step, carry):
        forward(lax.rem(mine + step, groups)).start()
        return carry

    lax.fori_loop(1, groups, send_tp, 0)
    own = pltpu.make_async_copy(land, gathered.at[mine], local_sem.at[1])
    own.start()

    def finish_tp(step, carry):
        forward(lax.rem(mine + step, groups)).wait_send()
        collected(lax.rem(mine + groups - step, groups)).wait_recv()
        return carry

    lax.fori_loop(1, groups, finish_tp, 0)
    own.wait()
    y_ref[...] = gathered[...]


def exchange_and_gather(x, collective):
    count = lax.axis_size("ctx")
    groups = lax.axis_size("tp")
    full = (groups,) + tuple(x.shape)
    return pl.pallas_call(
        _final_kernel,
        out_shape=jax.ShapeDtypeStruct(full, x.dtype),
        in_specs=[pl.BlockSpec(memory_space=pltpu.VMEM)],
        out_specs=pl.BlockSpec(memory_space=pltpu.VMEM),
        scratch_shapes=[
            pltpu.VMEM(x.shape, x.dtype),
            pltpu.VMEM(full, x.dtype),
            pltpu.SemaphoreType.DMA((count,)),
            pltpu.SemaphoreType.DMA((count,)),
            pltpu.SemaphoreType.DMA((groups,)),
            pltpu.SemaphoreType.DMA((groups,)),
            pltpu.SemaphoreType.DMA((2,)),
        ],
        compiler_params=pltpu.CompilerParams(collective_id=collective, has_side_effects=True),
    )(x)


def fourier_tables(length_all):
    split = 1 << (int(math.log2(length_all)) // 2)
    rows_hi = length_all // split
    scale = 2.0 * math.pi / length_all
    columns = jnp.arange(length_all, dtype=jnp.int32)
    low = jnp.arange(split, dtype=jnp.int32)
    high = jnp.arange(rows_hi, dtype=jnp.int32)
    angle_low = (low[:, None] * columns[None, :] % length_all).astype(jnp.float32) * scale
    angle_high = (split * high[:, None] * columns[None, :] % length_all).astype(jnp.float32) * scale
    cos_low, sin_low = jnp.cos(angle_low)[None], jnp.sin(angle_low)[None]
    cos_high, sin_high = jnp.cos(angle_high)[:, None], jnp.sin(angle_high)[:, None]
    cosine = (cos_high * cos_low - sin_high * sin_low).reshape(length_all, length_all)
    sine = (sin_high * cos_low + cos_high * sin_low).reshape(length_all, length_all)
    return lax.optimization_barrier((cosine.astype(jnp.bfloat16), sine.astype(jnp.bfloat16)))


def twist_tables(left_index, right_index, length_all):
    phase_index = left_index[:, None] * right_index[None, :] % length_all
    angles = phase_index.astype(jnp.float32) * (2.0 * math.pi / length_all)
    return (jnp.cos(angles), jnp.sin(angles))


def contract(form, left, right):
    return jnp.einsum(form, left, right, preferred_element_type=jnp.float32)


def local(k_feature, v_feature, q_feature, spectrum, skip_gain, out_weight):
    channels, tokens = k_feature.shape
    block_order = spectrum.shape[3]
    length_all = block_order * block_order
    ctx_count = lax.axis_size("ctx")
    tp_count = lax.axis_size("tp")
    slab_width = block_order // ctx_count
    rows_here = tokens // block_order
    half_rows = block_order // 2
    ctx_index = lax.axis_index("ctx")
    product = (k_feature.astype(jnp.float32) * v_feature.astype(jnp.float32)).astype(jnp.bfloat16)
    cosine_full, sine_full = fourier_tables(block_order)
    cosine_half = cosine_full[:half_rows]
    sine_half = sine_full[:half_rows]
    positions = jnp.arange(block_order, dtype=jnp.int32)
    local_ticks = ctx_index * slab_width + jnp.arange(slab_width, dtype=jnp.int32)

    both_rows = jnp.concatenate([product, q_feature], axis=0)
    outgoing = both_rows.reshape(2 * channels, rows_here, ctx_count, slab_width).transpose(2, 0, 1, 3)
    arrived = exchange(outgoing.reshape(ctx_count, 2 * channels, -1), "ctx", False, 0)
    arrived_rows = (
        arrived.reshape(ctx_count, 2 * channels, rows_here, slab_width)
        .transpose(1, 0, 2, 3)
        .reshape(2 * channels, half_rows, slab_width)
    )
    grid_rows, gate_rows = arrived_rows[:channels], arrived_rows[channels:]
    first_real = contract("cij,ia->caj", grid_rows, cosine_half)
    first_imag = -contract("cij,ia->caj", grid_rows, sine_half)
    twist_cosine, twist_sine = twist_tables(positions, local_ticks, length_all)
    spread_real = (first_real * twist_cosine + first_imag * twist_sine).astype(jnp.bfloat16)
    spread_imag = (first_imag * twist_cosine - first_real * twist_sine).astype(jnp.bfloat16)

    spread = jnp.stack([spread_real, spread_imag])
    outgoing = spread.reshape(2, channels, ctx_count, slab_width, slab_width).transpose(2, 0, 1, 3, 4)
    arrived = exchange(outgoing.reshape(ctx_count, -1, 128), "ctx", False, 1)
    block = (
        arrived.reshape(ctx_count, 2, channels, slab_width, slab_width)
        .transpose(1, 2, 3, 0, 4)
        .reshape(2, channels, slab_width, block_order)
    )
    block_real, block_imag = block[0], block[1]
    freq_real = contract("caj,jb->cab", block_real, cosine_full) + contract(
        "caj,jb->cab", block_imag, sine_full
    )
    freq_imag = contract("caj,jb->cab", block_imag, cosine_full) - contract(
        "caj,jb->cab", block_real, sine_full
    )
    resp_real = spectrum[0].astype(jnp.float32)
    resp_imag = spectrum[1].astype(jnp.float32)
    shaped_real = (freq_real * resp_real - freq_imag * resp_imag).astype(jnp.bfloat16)
    shaped_imag = (freq_real * resp_imag + freq_imag * resp_real).astype(jnp.bfloat16)
    inner_real = contract("cab,bj->caj", shaped_real, cosine_full) - contract(
        "cab,bj->caj", shaped_imag, sine_full
    )
    inner_imag = contract("cab,bj->caj", shaped_imag, cosine_full) + contract(
        "cab,bj->caj", shaped_real, sine_full
    )
    twist_cosine, twist_sine = twist_tables(local_ticks, positions, length_all)
    back_real = (inner_real * twist_cosine - inner_imag * twist_sine).astype(jnp.bfloat16)
    back_imag = (inner_imag * twist_cosine + inner_real * twist_sine).astype(jnp.bfloat16)

    back = jnp.stack([back_real, back_imag])
    outgoing = back.reshape(2, channels, slab_width, ctx_count, slab_width).transpose(3, 0, 1, 2, 4)
    arrived = exchange(outgoing.reshape(ctx_count, -1, 128), "ctx", False, 2)
    columns = (
        arrived.reshape(ctx_count, 2, channels, slab_width, slab_width)
        .transpose(1, 2, 0, 3, 4)
        .reshape(2, channels, block_order, slab_width)
    )
    summed = contract("ia,caj->cij", cosine_half, columns[0]) - contract(
        "ia,caj->cij", sine_half, columns[1]
    )
    spatial = (summed * (1.0 / length_all)).astype(jnp.bfloat16)
    gated = (
        gate_rows.astype(jnp.float32)
        * (spatial.astype(jnp.float32) + skip_gain[:, None, None] * grid_rows.astype(jnp.float32))
    ).astype(jnp.bfloat16)

    outgoing = gated.reshape(channels, ctx_count, rows_here, slab_width).transpose(1, 0, 2, 3)
    gathered = exchange_and_gather(outgoing.reshape(ctx_count, channels, -1), 3)
    outs_here = out_weight.shape[1] // tp_count
    tp_index = lax.axis_index("tp")
    my_weight = lax.dynamic_slice_in_dim(out_weight, tp_index * outs_here, outs_here, 1)
    mixed = contract(
        "sce,spck->epk", my_weight.reshape(tp_count, channels, outs_here), gathered
    )
    return (
        mixed.reshape(outs_here, ctx_count, rows_here, slab_width)
        .transpose(0, 2, 1, 3)
        .reshape(outs_here, tokens)
        .astype(jnp.bfloat16)
    )


def solution(mesh):
    placed = (
        P("tp", "ctx"),
        P("tp", "ctx"),
        P("tp", "ctx"),
        P(None, "tp", "ctx", None),
        P("tp"),
        P(),
    )
    return jax.shard_map(
        local, mesh=mesh, in_specs=placed, out_specs=P("tp", "ctx"), check_vma=False
    )
```

```python
import functools
import math

import jax
import jax.numpy as jnp
from jax import lax
from jax.experimental import pallas as pl
from jax.experimental.pallas import tpu as pltpu
from jax.sharding import PartitionSpec as P

MESH = pl.DeviceIdType.MESH


def _exchange_kernel(axis, gather, x_ref, y_ref, land, send_sem, recv_sem, local_sem):
    count = land.shape[0]
    me = lax.axis_index(axis)
    barrier = pltpu.get_barrier_semaphore()

    def greet(step, carry):
        peer = lax.rem(me + step, count)
        pl.semaphore_signal(barrier, 1, device_id={axis: peer}, device_id_type=MESH)
        return carry

    lax.fori_loop(1, count, greet, 0)
    pl.semaphore_wait(barrier, count - 1)

    def piece(peer):
        return x_ref if gather else x_ref.at[peer]

    def outgoing(peer):
        return pltpu.make_async_remote_copy(
            src_ref=piece(peer), dst_ref=land.at[me], send_sem=send_sem.at[peer],
            recv_sem=recv_sem.at[me], device_id={axis: peer}, device_id_type=MESH)

    def incoming(source):
        return pltpu.make_async_remote_copy(
            src_ref=piece(source), dst_ref=land.at[source], send_sem=send_sem.at[source],
            recv_sem=recv_sem.at[source], device_id={axis: source}, device_id_type=MESH)

    def send(step, carry):
        outgoing(lax.rem(me + step, count)).start()
        return carry

    lax.fori_loop(1, count, send, 0)
    local = pltpu.make_async_copy(piece(me), land.at[me], local_sem)
    local.start()

    def finish(step, carry):
        outgoing(lax.rem(me + step, count)).wait_send()
        incoming(lax.rem(me + count - step, count)).wait_recv()
        return carry

    lax.fori_loop(1, count, finish, 0)
    local.wait()
    y_ref[...] = land[...]


def exchange(x, axis, gather, collective):
    count = lax.axis_size(axis)
    chunk = x.shape if gather else x.shape[1:]
    full = (count,) + tuple(chunk)
    return pl.pallas_call(
        functools.partial(_exchange_kernel, axis, gather),
        out_shape=jax.ShapeDtypeStruct(full, x.dtype),
        in_specs=[pl.BlockSpec(memory_space=pltpu.VMEM)],
        out_specs=pl.BlockSpec(memory_space=pltpu.VMEM),
        scratch_shapes=[
            pltpu.VMEM(full, x.dtype),
            pltpu.SemaphoreType.DMA((count,)),
            pltpu.SemaphoreType.DMA((count,)),
            pltpu.SemaphoreType.DMA,
        ],
        compiler_params=pltpu.CompilerParams(collective_id=collective, has_side_effects=True),
    )(x)


def _final_kernel(x_ref, y_ref, land, gathered, send_sem, recv_sem, right_sem, left_sem, line_sem, local_sem):
    count = land.shape[0]
    groups = gathered.shape[0]
    me = lax.axis_index("ctx")
    mine = lax.axis_index("tp")
    has_right = mine < groups - 1
    has_left = mine > 0
    barrier = pltpu.get_barrier_semaphore()

    def greet(step, carry):
        peer = lax.rem(me + step, count)
        pl.semaphore_signal(barrier, 1, device_id={"ctx": peer}, device_id_type=MESH)
        return carry

    lax.fori_loop(1, count, greet, 0)

    @pl.when(has_right)
    def _():
        pl.semaphore_signal(barrier, 1, device_id={"tp": mine + 1}, device_id_type=MESH)

    @pl.when(has_left)
    def _():
        pl.semaphore_signal(barrier, 1, device_id={"tp": mine - 1}, device_id_type=MESH)

    pl.semaphore_wait(barrier, count - 1 + has_right.astype(jnp.int32) + has_left.astype(jnp.int32))

    def outgoing(peer):
        return pltpu.make_async_remote_copy(
            src_ref=x_ref.at[peer], dst_ref=land.at[me], send_sem=send_sem.at[peer],
            recv_sem=recv_sem.at[me], device_id={"ctx": peer}, device_id_type=MESH)

    def incoming(source):
        return pltpu.make_async_remote_copy(
            src_ref=x_ref.at[source], dst_ref=land.at[source], send_sem=send_sem.at[source],
            recv_sem=recv_sem.at[source], device_id={"ctx": source}, device_id_type=MESH)

    def send(step, carry):
        outgoing(lax.rem(me + step, count)).start()
        return carry

    lax.fori_loop(1, count, send, 0)
    local = pltpu.make_async_copy(x_ref.at[me], land.at[me], local_sem.at[0])
    local.start()

    def finish(step, carry):
        outgoing(lax.rem(me + step, count)).wait_send()
        incoming(lax.rem(me + count - step, count)).wait_recv()
        return carry

    lax.fori_loop(1, count, finish, 0)
    local.wait()
    own = pltpu.make_async_copy(land, gathered.at[mine], local_sem.at[1])
    own.start()
    own.wait()

    def to_right(slot):
        return pltpu.make_async_remote_copy(
            src_ref=gathered.at[slot], dst_ref=gathered.at[slot], send_sem=right_sem.at[slot],
            recv_sem=line_sem.at[slot], device_id={"tp": mine + 1}, device_id_type=MESH)

    def to_left(slot):
        return pltpu.make_async_remote_copy(
            src_ref=gathered.at[slot], dst_ref=gathered.at[slot], send_sem=left_sem.at[slot],
            recv_sem=line_sem.at[slot], device_id={"tp": mine - 1}, device_id_type=MESH)

    @pl.when(has_right)
    def _():
        to_right(mine).start()

    @pl.when(has_left)
    def _():
        to_left(mine).start()

    def relay(step, carry):
        @pl.when(step <= mine)
        def _():
            slot = mine - step
            to_right(slot).wait_recv()

            @pl.when(has_right)
            def _():
                to_right(slot).start()

        @pl.when(step < groups - mine)
        def _():
            slot = mine + step
            to_left(slot).wait_recv()

            @pl.when(has_left)
            def _():
                to_left(slot).start()

        return carry

    lax.fori_loop(1, groups, relay, 0)

    def drain(slot, carry):
        @pl.when(has_right & (slot <= mine))
        def _():
            to_right(slot).wait_send()

        @pl.when(has_left & (slot >= mine))
        def _():
            to_left(slot).wait_send()

        return carry

    lax.fori_loop(0, groups, drain, 0)
    y_ref[...] = gathered[...]


def exchange_and_gather(x, collective):
    count = lax.axis_size("ctx")
    groups = lax.axis_size("tp")
    full = (groups,) + tuple(x.shape)
    return pl.pallas_call(
        _final_kernel,
        out_shape=jax.ShapeDtypeStruct(full, x.dtype),
        in_specs=[pl.BlockSpec(memory_space=pltpu.VMEM)],
        out_specs=pl.BlockSpec(memory_space=pltpu.VMEM),
        scratch_shapes=[
            pltpu.VMEM(x.shape, x.dtype),
            pltpu.VMEM(full, x.dtype),
            pltpu.SemaphoreType.DMA((count,)),
            pltpu.SemaphoreType.DMA((count,)),
            pltpu.SemaphoreType.DMA((groups,)),
            pltpu.SemaphoreType.DMA((groups,)),
            pltpu.SemaphoreType.DMA((groups,)),
            pltpu.SemaphoreType.DMA((2,)),
        ],
        compiler_params=pltpu.CompilerParams(collective_id=collective, has_side_effects=True),
    )(x)


def fourier_tables(length_all):
    split = 1 << (int(math.log2(length_all)) // 2)
    rows_hi = length_all // split
    scale = 2.0 * math.pi / length_all
    columns = jnp.arange(length_all, dtype=jnp.int32)
    low = jnp.arange(split, dtype=jnp.int32)
    high = jnp.arange(rows_hi, dtype=jnp.int32)
    angle_low = (low[:, None] * columns[None, :] % length_all).astype(jnp.float32) * scale
    angle_high = (split * high[:, None] * columns[None, :] % length_all).astype(jnp.float32) * scale
    cos_low, sin_low = jnp.cos(angle_low)[None], jnp.sin(angle_low)[None]
    cos_high, sin_high = jnp.cos(angle_high)[:, None], jnp.sin(angle_high)[:, None]
    cosine = (cos_high * cos_low - sin_high * sin_low).reshape(length_all, length_all)
    sine = (sin_high * cos_low + cos_high * sin_low).reshape(length_all, length_all)
    return lax.optimization_barrier((cosine.astype(jnp.bfloat16), sine.astype(jnp.bfloat16)))


def twist_tables(left_index, right_index, length_all):
    phase_index = left_index[:, None] * right_index[None, :] % length_all
    angles = phase_index.astype(jnp.float32) * (2.0 * math.pi / length_all)
    return (jnp.cos(angles), jnp.sin(angles))


def contract(form, left, right):
    return jnp.einsum(form, left, right, preferred_element_type=jnp.float32)


def local(k_feature, v_feature, q_feature, spectrum, skip_gain, out_weight):
    channels, tokens = k_feature.shape
    block_order = spectrum.shape[3]
    length_all = block_order * block_order
    ctx_count = lax.axis_size("ctx")
    tp_count = lax.axis_size("tp")
    slab_width = block_order // ctx_count
    rows_here = tokens // block_order
    half_rows = block_order // 2
    ctx_index = lax.axis_index("ctx")
    product = (k_feature.astype(jnp.float32) * v_feature.astype(jnp.float32)).astype(jnp.bfloat16)
    cosine_full, sine_full = fourier_tables(block_order)
    cosine_half = cosine_full[:half_rows]
    sine_half = sine_full[:half_rows]
    positions = jnp.arange(block_order, dtype=jnp.int32)
    local_ticks = ctx_index * slab_width + jnp.arange(slab_width, dtype=jnp.int32)

    both_rows = jnp.concatenate([product, q_feature], axis=0)
    outgoing = both_rows.reshape(2 * channels, rows_here, ctx_count, slab_width).transpose(2, 0, 1, 3)
    arrived = exchange(outgoing.reshape(ctx_count, 2 * channels, -1), "ctx", False, 0)
    arrived_rows = (
        arrived.reshape(ctx_count, 2 * channels, rows_here, slab_width)
        .transpose(1, 0, 2, 3)
        .reshape(2 * channels, half_rows, slab_width)
    )
    grid_rows, gate_rows = arrived_rows[:channels], arrived_rows[channels:]
    first_real = contract("cij,ia->caj", grid_rows, cosine_half)
    first_imag = -contract("cij,ia->caj", grid_rows, sine_half)
    twist_cosine, twist_sine = twist_tables(positions, local_ticks, length_all)
    spread_real = (first_real * twist_cosine + first_imag * twist_sine).astype(jnp.bfloat16)
    spread_imag = (first_imag * twist_cosine - first_real * twist_sine).astype(jnp.bfloat16)

    spread = jnp.stack([spread_real, spread_imag])
    outgoing = spread.reshape(2, channels, ctx_count, slab_width, slab_width).transpose(2, 0, 1, 3, 4)
    arrived = exchange(outgoing.reshape(ctx_count, -1, 128), "ctx", False, 1)
    block = (
        arrived.reshape(ctx_count, 2, channels, slab_width, slab_width)
        .transpose(1, 2, 3, 0, 4)
        .reshape(2, channels, slab_width, block_order)
    )
    block_real, block_imag = block[0], block[1]
    freq_real = contract("caj,jb->cab", block_real, cosine_full) + contract(
        "caj,jb->cab", block_imag, sine_full
    )
    freq_imag = contract("caj,jb->cab", block_imag, cosine_full) - contract(
        "caj,jb->cab", block_real, sine_full
    )
    resp_real = spectrum[0].astype(jnp.float32)
    resp_imag = spectrum[1].astype(jnp.float32)
    shaped_real = (freq_real * resp_real - freq_imag * resp_imag).astype(jnp.bfloat16)
    shaped_imag = (freq_real * resp_imag + freq_imag * resp_real).astype(jnp.bfloat16)
    inner_real = contract("cab,bj->caj", shaped_real, cosine_full) - contract(
        "cab,bj->caj", shaped_imag, sine_full
    )
    inner_imag = contract("cab,bj->caj", shaped_imag, cosine_full) + contract(
        "cab,bj->caj", shaped_real, sine_full
    )
    twist_cosine, twist_sine = twist_tables(local_ticks, positions, length_all)
    back_real = (inner_real * twist_cosine - inner_imag * twist_sine).astype(jnp.bfloat16)
    back_imag = (inner_imag * twist_cosine + inner_real * twist_sine).astype(jnp.bfloat16)

    back = jnp.stack([back_real, back_imag])
    outgoing = back.reshape(2, channels, slab_width, ctx_count, slab_width).transpose(3, 0, 1, 2, 4)
    arrived = exchange(outgoing.reshape(ctx_count, -1, 128), "ctx", False, 2)
    columns = (
        arrived.reshape(ctx_count, 2, channels, slab_width, slab_width)
        .transpose(1, 2, 0, 3, 4)
        .reshape(2, channels, block_order, slab_width)
    )
    summed = contract("ia,caj->cij", cosine_half, columns[0]) - contract(
        "ia,caj->cij", sine_half, columns[1]
    )
    spatial = (summed * (1.0 / length_all)).astype(jnp.bfloat16)
    gated = (
        gate_rows.astype(jnp.float32)
        * (spatial.astype(jnp.float32) + skip_gain[:, None, None] * grid_rows.astype(jnp.float32))
    ).astype(jnp.bfloat16)

    outgoing = gated.reshape(channels, ctx_count, rows_here, slab_width).transpose(1, 0, 2, 3)
    gathered = exchange_and_gather(outgoing.reshape(ctx_count, channels, -1), 3)
    outs_here = out_weight.shape[1] // tp_count
    tp_index = lax.axis_index("tp")
    my_weight = lax.dynamic_slice_in_dim(out_weight, tp_index * outs_here, outs_here, 1)
    mixed = contract(
        "sce,spck->epk", my_weight.reshape(tp_count, channels, outs_here), gathered
    )
    return (
        mixed.reshape(outs_here, ctx_count, rows_here, slab_width)
        .transpose(0, 2, 1, 3)
        .reshape(outs_here, tokens)
        .astype(jnp.bfloat16)
    )


def solution(mesh):
    placed = (
        P("tp", "ctx"),
        P("tp", "ctx"),
        P("tp", "ctx"),
        P(None, "tp", "ctx", None),
        P("tp"),
        P(),
    )
    return jax.shard_map(
        local, mesh=mesh, in_specs=placed, out_specs=P("tp", "ctx"), check_vma=False
    )
```

```python
import functools
import math

import jax
import jax.numpy as jnp
from jax import lax
from jax.experimental import pallas as pl
from jax.experimental.pallas import tpu as pltpu
from jax.sharding import PartitionSpec as P

MESH = pl.DeviceIdType.MESH


def _exchange_kernel(axis, gather, x_ref, y_ref, land, send_sem, recv_sem, local_sem):
    count = land.shape[0]
    me = lax.axis_index(axis)
    barrier = pltpu.get_barrier_semaphore()

    def greet(step, carry):
        peer = lax.rem(me + step, count)
        pl.semaphore_signal(barrier, 1, device_id={axis: peer}, device_id_type=MESH)
        return carry

    lax.fori_loop(1, count, greet, 0)
    pl.semaphore_wait(barrier, count - 1)

    def piece(peer):
        return x_ref if gather else x_ref.at[peer]

    def outgoing(peer):
        return pltpu.make_async_remote_copy(
            src_ref=piece(peer), dst_ref=land.at[me], send_sem=send_sem.at[peer],
            recv_sem=recv_sem.at[me], device_id={axis: peer}, device_id_type=MESH)

    def incoming(source):
        return pltpu.make_async_remote_copy(
            src_ref=piece(source), dst_ref=land.at[source], send_sem=send_sem.at[source],
            recv_sem=recv_sem.at[source], device_id={axis: source}, device_id_type=MESH)

    def send(step, carry):
        outgoing(lax.rem(me + step, count)).start()
        return carry

    lax.fori_loop(1, count, send, 0)
    local = pltpu.make_async_copy(piece(me), land.at[me], local_sem)
    local.start()

    def finish(step, carry):
        outgoing(lax.rem(me + step, count)).wait_send()
        incoming(lax.rem(me + count - step, count)).wait_recv()
        return carry

    lax.fori_loop(1, count, finish, 0)
    local.wait()
    y_ref[...] = land[...]


def exchange(x, axis, gather, collective):
    count = lax.axis_size(axis)
    chunk = x.shape if gather else x.shape[1:]
    full = (count,) + tuple(chunk)
    return pl.pallas_call(
        functools.partial(_exchange_kernel, axis, gather),
        out_shape=jax.ShapeDtypeStruct(full, x.dtype),
        in_specs=[pl.BlockSpec(memory_space=pltpu.VMEM)],
        out_specs=pl.BlockSpec(memory_space=pltpu.VMEM),
        scratch_shapes=[
            pltpu.VMEM(full, x.dtype),
            pltpu.SemaphoreType.DMA((count,)),
            pltpu.SemaphoreType.DMA((count,)),
            pltpu.SemaphoreType.DMA,
        ],
        compiler_params=pltpu.CompilerParams(collective_id=collective, has_side_effects=True),
    )(x)


def fourier_tables(length_all):
    split = 1 << (int(math.log2(length_all)) // 2)
    rows_hi = length_all // split
    scale = 2.0 * math.pi / length_all
    columns = jnp.arange(length_all, dtype=jnp.int32)
    low = jnp.arange(split, dtype=jnp.int32)
    high = jnp.arange(rows_hi, dtype=jnp.int32)
    angle_low = (low[:, None] * columns[None, :] % length_all).astype(jnp.float32) * scale
    angle_high = (split * high[:, None] * columns[None, :] % length_all).astype(jnp.float32) * scale
    cos_low, sin_low = jnp.cos(angle_low)[None], jnp.sin(angle_low)[None]
    cos_high, sin_high = jnp.cos(angle_high)[:, None], jnp.sin(angle_high)[:, None]
    cosine = (cos_high * cos_low - sin_high * sin_low).reshape(length_all, length_all)
    sine = (sin_high * cos_low + cos_high * sin_low).reshape(length_all, length_all)
    return lax.optimization_barrier((cosine.astype(jnp.bfloat16), sine.astype(jnp.bfloat16)))


def twist_tables(left_index, right_index, length_all):
    phase_index = left_index[:, None] * right_index[None, :] % length_all
    angles = phase_index.astype(jnp.float32) * (2.0 * math.pi / length_all)
    return (jnp.cos(angles), jnp.sin(angles))


def contract(form, left, right):
    return jnp.einsum(form, left, right, preferred_element_type=jnp.float32)


def local(k_feature, v_feature, q_feature, spectrum, skip_gain, out_weight):
    channels, tokens = k_feature.shape
    block_order = spectrum.shape[3]
    length_all = block_order * block_order
    ctx_count = lax.axis_size("ctx")
    tp_count = lax.axis_size("tp")
    slab_width = block_order // ctx_count
    rows_here = tokens // block_order
    half_rows = block_order // 2
    ctx_index = lax.axis_index("ctx")
    product = (k_feature.astype(jnp.float32) * v_feature.astype(jnp.float32)).astype(jnp.bfloat16)
    cosine_full, sine_full = fourier_tables(block_order)
    cosine_half = cosine_full[:half_rows]
    sine_half = sine_full[:half_rows]
    positions = jnp.arange(block_order, dtype=jnp.int32)
    local_ticks = ctx_index * slab_width + jnp.arange(slab_width, dtype=jnp.int32)

    outgoing = product.reshape(channels, rows_here, ctx_count, slab_width).transpose(2, 0, 1, 3)
    arrived = exchange(outgoing.reshape(ctx_count, channels, -1), "ctx", False, 0)
    grid_rows = (
        arrived.reshape(ctx_count, channels, rows_here, slab_width)
        .transpose(1, 0, 2, 3)
        .reshape(channels, half_rows, slab_width)
    )
    both_full = jnp.stack([cosine_full, sine_full])
    both_half = jnp.stack([cosine_half, sine_half])
    first = contract("sia,cij->scaj", both_half, grid_rows)
    twist_cosine, twist_sine = twist_tables(positions, local_ticks, length_all)
    spread = jnp.stack(
        [
            first[0] * twist_cosine - first[1] * twist_sine,
            -first[1] * twist_cosine - first[0] * twist_sine,
        ]
    ).astype(jnp.bfloat16)

    outgoing = spread.reshape(2, channels, ctx_count, slab_width, slab_width).transpose(2, 0, 1, 3, 4)
    arrived = exchange(outgoing.reshape(ctx_count, -1, 128), "ctx", False, 1)
    block = (
        arrived.reshape(ctx_count, 2, channels, slab_width, slab_width)
        .transpose(1, 2, 3, 0, 4)
        .reshape(2, channels, slab_width, block_order)
    )
    freq = contract("rcaj,sjb->srcab", block, both_full)
    freq_real = freq[0, 0] + freq[1, 1]
    freq_imag = freq[0, 1] - freq[1, 0]
    resp_real = spectrum[0].astype(jnp.float32)
    resp_imag = spectrum[1].astype(jnp.float32)
    shaped = jnp.stack(
        [
            freq_real * resp_real - freq_imag * resp_imag,
            freq_real * resp_imag + freq_imag * resp_real,
        ]
    ).astype(jnp.bfloat16)
    inner = contract("rcab,sbj->srcaj", shaped, both_full)
    inner_real = inner[0, 0] - inner[1, 1]
    inner_imag = inner[0, 1] + inner[1, 0]
    twist_cosine, twist_sine = twist_tables(local_ticks, positions, length_all)
    back = jnp.stack(
        [
            inner_real * twist_cosine - inner_imag * twist_sine,
            inner_imag * twist_cosine + inner_real * twist_sine,
        ]
    ).astype(jnp.bfloat16)

    outgoing = back.reshape(2, channels, slab_width, ctx_count, slab_width).transpose(3, 0, 1, 2, 4)
    arrived = exchange(outgoing.reshape(ctx_count, -1, 128), "ctx", False, 2)
    columns = (
        arrived.reshape(ctx_count, 2, channels, slab_width, slab_width)
        .transpose(1, 2, 0, 3, 4)
        .reshape(2, channels, block_order, slab_width)
    )
    parts = contract("sia,rcaj->srcij", both_half, columns)
    summed = parts[0, 0] - parts[1, 1]
    spatial = (summed * (1.0 / length_all)).astype(jnp.bfloat16)

    outgoing = spatial.reshape(channels, ctx_count, rows_here, slab_width).transpose(1, 0, 2, 3)
    arrived = exchange(outgoing.reshape(ctx_count, channels, -1), "ctx", False, 3)
    convolved = (
        arrived.reshape(ctx_count, channels, rows_here, slab_width)
        .transpose(1, 2, 0, 3)
        .reshape(channels, tokens)
    )
    gated_rows = (
        q_feature.astype(jnp.float32)
        * (convolved.astype(jnp.float32) + skip_gain[:, None] * product.astype(jnp.float32))
    ).astype(jnp.bfloat16)
    gated_all = exchange(gated_rows, "tp", True, 4).reshape(tp_count * channels, tokens)
    outs_here = out_weight.shape[1] // tp_count
    tp_index = lax.axis_index("tp")
    my_weight = lax.dynamic_slice_in_dim(out_weight, tp_index * outs_here, outs_here, 1)
    return jnp.dot(my_weight.T, gated_all, preferred_element_type=jnp.float32).astype(jnp.bfloat16)


def solution(mesh):
    placed = (
        P("tp", "ctx"),
        P("tp", "ctx"),
        P("tp", "ctx"),
        P(None, "tp", "ctx", None),
        P("tp"),
        P(),
    )
    return jax.shard_map(
        local, mesh=mesh, in_specs=placed, out_specs=P("tp", "ctx"), check_vma=False
    )
```

```python
import functools
import math

import jax
import jax.numpy as jnp
from jax import lax
from jax.experimental import pallas as pl
from jax.experimental.pallas import tpu as pltpu
from jax.sharding import PartitionSpec as P

MESH = pl.DeviceIdType.MESH


def _exchange_kernel(axis, gather, x_ref, y_ref, land, send_sem, recv_sem, local_sem):
    count = land.shape[0]
    me = lax.rem(lax.axis_index(axis), count)
    base = lax.axis_index(axis) - me
    barrier = pltpu.get_barrier_semaphore()

    def greet(step, carry):
        peer = lax.rem(me + step, count)
        pl.semaphore_signal(barrier, 1, device_id={axis: base + peer}, device_id_type=MESH)
        return carry

    lax.fori_loop(1, count, greet, 0)
    pl.semaphore_wait(barrier, count - 1)

    def piece(peer):
        return x_ref if gather else x_ref.at[peer]

    def outgoing(peer):
        return pltpu.make_async_remote_copy(
            src_ref=piece(peer), dst_ref=land.at[me], send_sem=send_sem.at[peer],
            recv_sem=recv_sem.at[me], device_id={axis: base + peer}, device_id_type=MESH)

    def incoming(source):
        return pltpu.make_async_remote_copy(
            src_ref=piece(source), dst_ref=land.at[source], send_sem=send_sem.at[source],
            recv_sem=recv_sem.at[source], device_id={axis: base + source}, device_id_type=MESH)

    def send(step, carry):
        outgoing(lax.rem(me + step, count)).start()
        return carry

    lax.fori_loop(1, count, send, 0)
    local = pltpu.make_async_copy(piece(me), land.at[me], local_sem)
    local.start()

    def finish(step, carry):
        outgoing(lax.rem(me + step, count)).wait_send()
        incoming(lax.rem(me + count - step, count)).wait_recv()
        return carry

    lax.fori_loop(1, count, finish, 0)
    local.wait()
    y_ref[...] = land[...]


def exchange(x, axis, gather, collective):
    count = lax.axis_size(axis) if gather else x.shape[0]
    chunk = x.shape if gather else x.shape[1:]
    full = (count,) + tuple(chunk)
    return pl.pallas_call(
        functools.partial(_exchange_kernel, axis, gather),
        out_shape=jax.ShapeDtypeStruct(full, x.dtype),
        in_specs=[pl.BlockSpec(memory_space=pltpu.VMEM)],
        out_specs=pl.BlockSpec(memory_space=pltpu.VMEM),
        scratch_shapes=[
            pltpu.VMEM(full, x.dtype),
            pltpu.SemaphoreType.DMA((count,)),
            pltpu.SemaphoreType.DMA((count,)),
            pltpu.SemaphoreType.DMA,
        ],
        compiler_params=pltpu.CompilerParams(collective_id=collective, has_side_effects=True),
    )(x)


def fourier_tables(length_all):
    split = 1 << (int(math.log2(length_all)) // 2)
    rows_hi = length_all // split
    scale = 2.0 * math.pi / length_all
    columns = jnp.arange(length_all, dtype=jnp.int32)
    low = jnp.arange(split, dtype=jnp.int32)
    high = jnp.arange(rows_hi, dtype=jnp.int32)
    angle_low = (low[:, None] * columns[None, :] % length_all).astype(jnp.float32) * scale
    angle_high = (split * high[:, None] * columns[None, :] % length_all).astype(jnp.float32) * scale
    cos_low, sin_low = jnp.cos(angle_low)[None], jnp.sin(angle_low)[None]
    cos_high, sin_high = jnp.cos(angle_high)[:, None], jnp.sin(angle_high)[:, None]
    cosine = (cos_high * cos_low - sin_high * sin_low).reshape(length_all, length_all)
    sine = (sin_high * cos_low + cos_high * sin_low).reshape(length_all, length_all)
    return lax.optimization_barrier((cosine.astype(jnp.bfloat16), sine.astype(jnp.bfloat16)))


def twist_tables(left_index, right_index, length_all):
    phase_index = left_index[:, None] * right_index[None, :] % length_all
    angles = phase_index.astype(jnp.float32) * (2.0 * math.pi / length_all)
    return (jnp.cos(angles), jnp.sin(angles))


def contract(form, left, right):
    return jnp.einsum(form, left, right, preferred_element_type=jnp.float32)


def local(k_feature, v_feature, q_feature, spectrum, skip_gain, out_weight):
    channels, tokens = k_feature.shape
    block_order = spectrum.shape[3]
    length_all = block_order * block_order
    ctx_count = lax.axis_size("ctx")
    tp_count = lax.axis_size("tp")
    halves = 2
    group = ctx_count // halves
    slab = block_order // group
    freq_rows = block_order // ctx_count
    half_freqs = block_order // halves
    rows_here = tokens // block_order
    half_rows = block_order // 2
    ctx_index = lax.axis_index("ctx")
    half_index = ctx_index // group
    group_index = ctx_index - half_index * group
    product = (k_feature.astype(jnp.float32) * v_feature.astype(jnp.float32)).astype(jnp.bfloat16)
    cosine_full, sine_full = fourier_tables(block_order)
    both_full = jnp.stack([cosine_full, sine_full])
    both_sub = lax.dynamic_slice_in_dim(both_full[:, :half_rows], half_index * half_freqs, half_freqs, 2)
    my_freqs = half_index * half_freqs + jnp.arange(half_freqs, dtype=jnp.int32)
    my_columns = group_index * slab + jnp.arange(slab, dtype=jnp.int32)
    local_ticks = ctx_index * freq_rows + jnp.arange(freq_rows, dtype=jnp.int32)
    positions = jnp.arange(block_order, dtype=jnp.int32)

    outgoing = product.reshape(channels, rows_here, group, slab).transpose(2, 0, 1, 3)
    outgoing = jnp.broadcast_to(outgoing[None], (halves,) + outgoing.shape)
    arrived = exchange(outgoing.reshape(ctx_count, channels, -1), "ctx", False, 0)
    grid_rows = (
        arrived.reshape(ctx_count, channels, rows_here, slab)
        .transpose(1, 0, 2, 3)
        .reshape(channels, half_rows, slab)
    )
    first = contract("sia,cij->scaj", both_sub, grid_rows)
    twist_cosine, twist_sine = twist_tables(my_freqs, my_columns, length_all)
    spread = jnp.stack(
        [
            first[0] * twist_cosine - first[1] * twist_sine,
            -first[1] * twist_cosine - first[0] * twist_sine,
        ]
    ).astype(jnp.bfloat16)

    outgoing = spread.reshape(2, channels, group, freq_rows, slab).transpose(2, 0, 1, 3, 4)
    arrived = exchange(outgoing.reshape(group, -1, 128), "ctx", False, 1)
    block = (
        arrived.reshape(group, 2, channels, freq_rows, slab)
        .transpose(1, 2, 3, 0, 4)
        .reshape(2, channels, freq_rows, block_order)
    )
    freq = contract("rcaj,sjb->srcab", block, both_full)
    freq_real = freq[0, 0] + freq[1, 1]
    freq_imag = freq[0, 1] - freq[1, 0]
    resp_real = spectrum[0].astype(jnp.float32)
    resp_imag = spectrum[1].astype(jnp.float32)
    shaped = jnp.stack(
        [
            freq_real * resp_real - freq_imag * resp_imag,
            freq_real * resp_imag + freq_imag * resp_real,
        ]
    ).astype(jnp.bfloat16)
    inner = contract("rcab,sbj->srcaj", shaped, both_full)
    inner_real = inner[0, 0] - inner[1, 1]
    inner_imag = inner[0, 1] + inner[1, 0]
    twist_cosine, twist_sine = twist_tables(local_ticks, positions, length_all)
    back = jnp.stack(
        [
            inner_real * twist_cosine - inner_imag * twist_sine,
            inner_imag * twist_cosine + inner_real * twist_sine,
        ]
    ).astype(jnp.bfloat16)

    outgoing = back.reshape(2, channels, freq_rows, group, slab).transpose(3, 0, 1, 2, 4)
    arrived = exchange(outgoing.reshape(group, -1, 128), "ctx", False, 2)
    columns = (
        arrived.reshape(group, 2, channels, freq_rows, slab)
        .transpose(1, 2, 0, 3, 4)
        .reshape(2, channels, half_freqs, slab)
    )
    parts = contract("sia,rcaj->srcij", both_sub, columns)
    partial = ((parts[0, 0] - parts[1, 1]) * (1.0 / length_all)).astype(jnp.bfloat16)

    outgoing = partial.reshape(channels, ctx_count, rows_here, slab).transpose(1, 0, 2, 3)
    arrived = exchange(outgoing.reshape(ctx_count, channels, -1), "ctx", False, 3)
    convolved = (
        arrived.reshape(halves, group, channels, rows_here, slab)
        .astype(jnp.float32)
        .sum(0)
        .transpose(1, 2, 0, 3)
        .reshape(channels, tokens)
        .astype(jnp.bfloat16)
    )
    gated_rows = (
        q_feature.astype(jnp.float32)
        * (convolved.astype(jnp.float32) + skip_gain[:, None] * product.astype(jnp.float32))
    ).astype(jnp.bfloat16)
    gated_all = exchange(gated_rows, "tp", True, 4).reshape(tp_count * channels, tokens)
    outs_here = out_weight.shape[1] // tp_count
    tp_index = lax.axis_index("tp")
    my_weight = lax.dynamic_slice_in_dim(out_weight, tp_index * outs_here, outs_here, 1)
    return jnp.dot(my_weight.T, gated_all, preferred_element_type=jnp.float32).astype(jnp.bfloat16)


def solution(mesh):
    placed = (
        P("tp", "ctx"),
        P("tp", "ctx"),
        P("tp", "ctx"),
        P(None, "tp", "ctx", None),
        P("tp"),
        P(),
    )
    return jax.shard_map(
        local, mesh=mesh, in_specs=placed, out_specs=P("tp", "ctx"), check_vma=False
    )
```

```python
import functools
import math

import jax
import jax.numpy as jnp
from jax import lax
from jax.experimental import pallas as pl
from jax.experimental.pallas import tpu as pltpu
from jax.sharding import PartitionSpec as P

MESH = pl.DeviceIdType.MESH


def _exchange_kernel(axis, gather, x_ref, y_ref, land, send_sem, recv_sem, local_sem):
    count = land.shape[0]
    me = lax.rem(lax.axis_index(axis), count)
    base = lax.axis_index(axis) - me
    barrier = pltpu.get_barrier_semaphore()

    def greet(step, carry):
        peer = lax.rem(me + step, count)
        pl.semaphore_signal(barrier, 1, device_id={axis: base + peer}, device_id_type=MESH)
        return carry

    lax.fori_loop(1, count, greet, 0)
    pl.semaphore_wait(barrier, count - 1)

    def piece(peer):
        return x_ref if gather else x_ref.at[lax.rem(peer, x_ref.shape[0])]

    def outgoing(peer):
        return pltpu.make_async_remote_copy(
            src_ref=piece(peer), dst_ref=land.at[me], send_sem=send_sem.at[peer],
            recv_sem=recv_sem.at[me], device_id={axis: base + peer}, device_id_type=MESH)

    def incoming(source):
        return pltpu.make_async_remote_copy(
            src_ref=piece(source), dst_ref=land.at[source], send_sem=send_sem.at[source],
            recv_sem=recv_sem.at[source], device_id={axis: base + source}, device_id_type=MESH)

    def send(step, carry):
        outgoing(lax.rem(me + step, count)).start()
        return carry

    lax.fori_loop(1, count, send, 0)
    local = pltpu.make_async_copy(piece(me), land.at[me], local_sem)
    local.start()

    def finish(step, carry):
        outgoing(lax.rem(me + step, count)).wait_send()
        incoming(lax.rem(me + count - step, count)).wait_recv()
        return carry

    lax.fori_loop(1, count, finish, 0)
    local.wait()
    y_ref[...] = land[...]


def exchange(x, axis, gather, collective, count=None):
    count = count or (lax.axis_size(axis) if gather else x.shape[0])
    chunk = x.shape if gather else x.shape[1:]
    full = (count,) + tuple(chunk)
    return pl.pallas_call(
        functools.partial(_exchange_kernel, axis, gather),
        out_shape=jax.ShapeDtypeStruct(full, x.dtype),
        in_specs=[pl.BlockSpec(memory_space=pltpu.VMEM)],
        out_specs=pl.BlockSpec(memory_space=pltpu.VMEM),
        scratch_shapes=[
            pltpu.VMEM(full, x.dtype),
            pltpu.SemaphoreType.DMA((count,)),
            pltpu.SemaphoreType.DMA((count,)),
            pltpu.SemaphoreType.DMA,
        ],
        compiler_params=pltpu.CompilerParams(collective_id=collective, has_side_effects=True),
    )(x)


def fourier_tables(length_all):
    split = 1 << (int(math.log2(length_all)) // 2)
    rows_hi = length_all // split
    scale = 2.0 * math.pi / length_all
    columns = jnp.arange(length_all, dtype=jnp.int32)
    low = jnp.arange(split, dtype=jnp.int32)
    high = jnp.arange(rows_hi, dtype=jnp.int32)
    angle_low = (low[:, None] * columns[None, :] % length_all).astype(jnp.float32) * scale
    angle_high = (split * high[:, None] * columns[None, :] % length_all).astype(jnp.float32) * scale
    cos_low, sin_low = jnp.cos(angle_low)[None], jnp.sin(angle_low)[None]
    cos_high, sin_high = jnp.cos(angle_high)[:, None], jnp.sin(angle_high)[:, None]
    cosine = (cos_high * cos_low - sin_high * sin_low).reshape(length_all, length_all)
    sine = (sin_high * cos_low + cos_high * sin_low).reshape(length_all, length_all)
    return lax.optimization_barrier((cosine.astype(jnp.bfloat16), sine.astype(jnp.bfloat16)))


def twist_tables(left_index, right_index, length_all):
    phase_index = left_index[:, None] * right_index[None, :] % length_all
    angles = phase_index.astype(jnp.float32) * (2.0 * math.pi / length_all)
    return (jnp.cos(angles), jnp.sin(angles))


def contract(form, left, right):
    return jnp.einsum(form, left, right, preferred_element_type=jnp.float32)


def local(k_feature, v_feature, q_feature, spectrum, skip_gain, out_weight):
    channels, tokens = k_feature.shape
    block_order = spectrum.shape[3]
    length_all = block_order * block_order
    ctx_count = lax.axis_size("ctx")
    tp_count = lax.axis_size("tp")
    halves = 2
    group = ctx_count // halves
    slab = block_order // group
    freq_rows = block_order // ctx_count
    half_freqs = block_order // halves
    rows_here = tokens // block_order
    half_rows = block_order // 2
    ctx_index = lax.axis_index("ctx")
    half_index = ctx_index // group
    group_index = ctx_index - half_index * group
    product = (k_feature.astype(jnp.float32) * v_feature.astype(jnp.float32)).astype(jnp.bfloat16)
    cosine_full, sine_full = fourier_tables(block_order)
    both_full = jnp.stack([cosine_full, sine_full])
    both_sub = lax.dynamic_slice_in_dim(both_full[:, :half_rows], half_index * half_freqs, half_freqs, 2)
    my_freqs = half_index * half_freqs + jnp.arange(half_freqs, dtype=jnp.int32)
    my_columns = group_index * slab + jnp.arange(slab, dtype=jnp.int32)
    local_ticks = ctx_index * freq_rows + jnp.arange(freq_rows, dtype=jnp.int32)
    positions = jnp.arange(block_order, dtype=jnp.int32)

    outgoing = product.reshape(channels, rows_here, group, slab).transpose(2, 0, 1, 3)
    arrived = exchange(outgoing.reshape(group, channels, -1), "ctx", False, 0, ctx_count)
    grid_rows = (
        arrived.reshape(ctx_count, channels, rows_here, slab)
        .transpose(1, 0, 2, 3)
        .reshape(channels, half_rows, slab)
    )
    first = contract("sia,cij->scaj", both_sub, grid_rows)
    twist_cosine, twist_sine = twist_tables(my_freqs, my_columns, length_all)
    spread = jnp.stack(
        [
            first[0] * twist_cosine - first[1] * twist_sine,
            -first[1] * twist_cosine - first[0] * twist_sine,
        ]
    ).astype(jnp.bfloat16)

    outgoing = spread.reshape(2, channels, group, freq_rows, slab).transpose(2, 0, 1, 3, 4)
    arrived = exchange(outgoing.reshape(group, -1, 128), "ctx", False, 1)
    block = (
        arrived.reshape(group, 2, channels, freq_rows, slab)
        .transpose(1, 2, 3, 0, 4)
        .reshape(2, channels, freq_rows, block_order)
    )
    freq = contract("rcaj,sjb->srcab", block, both_full)
    freq_real = freq[0, 0] + freq[1, 1]
    freq_imag = freq[0, 1] - freq[1, 0]
    resp_real = spectrum[0].astype(jnp.float32)
    resp_imag = spectrum[1].astype(jnp.float32)
    shaped = jnp.stack(
        [
            freq_real * resp_real - freq_imag * resp_imag,
            freq_real * resp_imag + freq_imag * resp_real,
        ]
    ).astype(jnp.bfloat16)
    inner = contract("rcab,sbj->srcaj", shaped, both_full)
    inner_real = inner[0, 0] - inner[1, 1]
    inner_imag = inner[0, 1] + inner[1, 0]
    twist_cosine, twist_sine = twist_tables(local_ticks, positions, length_all)
    back = jnp.stack(
        [
            inner_real * twist_cosine - inner_imag * twist_sine,
            inner_imag * twist_cosine + inner_real * twist_sine,
        ]
    ).astype(jnp.bfloat16)

    outgoing = back.reshape(2, channels, freq_rows, group, slab).transpose(3, 0, 1, 2, 4)
    arrived = exchange(outgoing.reshape(group, -1, 128), "ctx", False, 2)
    columns = (
        arrived.reshape(group, 2, channels, freq_rows, slab)
        .transpose(1, 2, 0, 3, 4)
        .reshape(2, channels, half_freqs, slab)
    )
    parts = contract("sia,rcaj->srcij", both_sub, columns)
    partial = ((parts[0, 0] - parts[1, 1]) * (1.0 / length_all)).astype(jnp.bfloat16)

    outgoing = partial.reshape(channels, ctx_count, rows_here, slab).transpose(1, 0, 2, 3)
    arrived = exchange(outgoing.reshape(ctx_count, channels, -1), "ctx", False, 3)
    convolved = (
        arrived.reshape(halves, group, channels, rows_here, slab)
        .astype(jnp.float32)
        .sum(0)
        .transpose(1, 2, 0, 3)
        .reshape(channels, tokens)
        .astype(jnp.bfloat16)
    )
    gated_rows = (
        q_feature.astype(jnp.float32)
        * (convolved.astype(jnp.float32) + skip_gain[:, None] * product.astype(jnp.float32))
    ).astype(jnp.bfloat16)
    gated_all = exchange(gated_rows, "tp", True, 4).reshape(tp_count * channels, tokens)
    outs_here = out_weight.shape[1] // tp_count
    tp_index = lax.axis_index("tp")
    my_weight = lax.dynamic_slice_in_dim(out_weight, tp_index * outs_here, outs_here, 1)
    return jnp.dot(my_weight.T, gated_all, preferred_element_type=jnp.float32).astype(jnp.bfloat16)


def solution(mesh):
    placed = (
        P("tp", "ctx"),
        P("tp", "ctx"),
        P("tp", "ctx"),
        P(None, "tp", "ctx", None),
        P("tp"),
        P(),
    )
    return jax.shard_map(
        local, mesh=mesh, in_specs=placed, out_specs=P("tp", "ctx"), check_vma=False
    )
```

```python
import functools
import math

import jax
import jax.numpy as jnp
from jax import lax
from jax.experimental import pallas as pl
from jax.experimental.pallas import tpu as pltpu
from jax.sharding import PartitionSpec as P

MESH = pl.DeviceIdType.MESH


def _exchange_kernel(axis, gather, x_ref, y_ref, land, send_sem, recv_sem, local_sem):
    count = land.shape[0]
    me = lax.rem(lax.axis_index(axis), count)
    base = lax.axis_index(axis) - me
    barrier = pltpu.get_barrier_semaphore()

    def greet(step, carry):
        peer = lax.rem(me + step, count)
        pl.semaphore_signal(barrier, 1, device_id={axis: base + peer}, device_id_type=MESH)
        return carry

    lax.fori_loop(1, count, greet, 0)
    pl.semaphore_wait(barrier, count - 1)

    def piece(peer):
        return x_ref if gather else x_ref.at[lax.rem(peer, x_ref.shape[0])]

    def outgoing(peer):
        return pltpu.make_async_remote_copy(
            src_ref=piece(peer), dst_ref=land.at[me], send_sem=send_sem.at[peer],
            recv_sem=recv_sem.at[me], device_id={axis: base + peer}, device_id_type=MESH)

    def incoming(source):
        return pltpu.make_async_remote_copy(
            src_ref=piece(source), dst_ref=land.at[source], send_sem=send_sem.at[source],
            recv_sem=recv_sem.at[source], device_id={axis: base + source}, device_id_type=MESH)

    def send(step, carry):
        outgoing(lax.rem(me + step, count)).start()
        return carry

    lax.fori_loop(1, count, send, 0)
    local = pltpu.make_async_copy(piece(me), land.at[me], local_sem)
    local.start()

    def finish(step, carry):
        outgoing(lax.rem(me + step, count)).wait_send()
        incoming(lax.rem(me + count - step, count)).wait_recv()
        return carry

    lax.fori_loop(1, count, finish, 0)
    local.wait()
    y_ref[...] = land[...]


def exchange(x, axis, gather, collective, count=None):
    count = count or (lax.axis_size(axis) if gather else x.shape[0])
    chunk = x.shape if gather else x.shape[1:]
    full = (count,) + tuple(chunk)
    return pl.pallas_call(
        functools.partial(_exchange_kernel, axis, gather),
        out_shape=jax.ShapeDtypeStruct(full, x.dtype),
        in_specs=[pl.BlockSpec(memory_space=pltpu.VMEM)],
        out_specs=pl.BlockSpec(memory_space=pltpu.VMEM),
        scratch_shapes=[
            pltpu.VMEM(full, x.dtype),
            pltpu.SemaphoreType.DMA((count,)),
            pltpu.SemaphoreType.DMA((count,)),
            pltpu.SemaphoreType.DMA,
        ],
        compiler_params=pltpu.CompilerParams(collective_id=collective, has_side_effects=True),
    )(x)


def fourier_tables(length_all):
    split = 1 << (int(math.log2(length_all)) // 2)
    rows_hi = length_all // split
    scale = 2.0 * math.pi / length_all
    columns = jnp.arange(length_all, dtype=jnp.int32)
    low = jnp.arange(split, dtype=jnp.int32)
    high = jnp.arange(rows_hi, dtype=jnp.int32)
    angle_low = (low[:, None] * columns[None, :] % length_all).astype(jnp.float32) * scale
    angle_high = (split * high[:, None] * columns[None, :] % length_all).astype(jnp.float32) * scale
    cos_low, sin_low = jnp.cos(angle_low)[None], jnp.sin(angle_low)[None]
    cos_high, sin_high = jnp.cos(angle_high)[:, None], jnp.sin(angle_high)[:, None]
    cosine = (cos_high * cos_low - sin_high * sin_low).reshape(length_all, length_all)
    sine = (sin_high * cos_low + cos_high * sin_low).reshape(length_all, length_all)
    return lax.optimization_barrier((cosine.astype(jnp.bfloat16), sine.astype(jnp.bfloat16)))


def twist_tables(left_index, right_index, length_all):
    phase_index = left_index[:, None] * right_index[None, :] % length_all
    angles = phase_index.astype(jnp.float32) * (2.0 * math.pi / length_all)
    return (jnp.cos(angles), jnp.sin(angles))


def contract(form, left, right):
    return jnp.einsum(form, left, right, preferred_element_type=jnp.float32)


def local(k_feature, v_feature, q_feature, spectrum, skip_gain, out_weight):
    channels, tokens = k_feature.shape
    block_order = spectrum.shape[3]
    length_all = block_order * block_order
    ctx_count = lax.axis_size("ctx")
    tp_count = lax.axis_size("tp")
    halves = 2
    group = ctx_count // halves
    slab = block_order // group
    freq_rows = block_order // ctx_count
    half_freqs = block_order // halves
    rows_here = tokens // block_order
    half_rows = block_order // 2
    ctx_index = lax.axis_index("ctx")
    half_index = ctx_index // group
    group_index = ctx_index - half_index * group
    product = (k_feature.astype(jnp.float32) * v_feature.astype(jnp.float32)).astype(jnp.bfloat16)
    cosine_full, sine_full = fourier_tables(block_order)
    both_full = jnp.stack([cosine_full, sine_full])
    both_sub = lax.dynamic_slice_in_dim(both_full[:, :half_rows], half_index * half_freqs, half_freqs, 2)
    my_freqs = half_index * half_freqs + jnp.arange(half_freqs, dtype=jnp.int32)
    my_columns = group_index * slab + jnp.arange(slab, dtype=jnp.int32)
    local_ticks = ctx_index * freq_rows + jnp.arange(freq_rows, dtype=jnp.int32)
    positions = jnp.arange(block_order, dtype=jnp.int32)

    outgoing = product.reshape(channels, rows_here, group, slab).transpose(2, 0, 1, 3)
    arrived = exchange(outgoing.reshape(group, channels, -1), "ctx", False, 0, ctx_count)
    grid_rows = (
        arrived.reshape(ctx_count, channels, rows_here, slab)
        .transpose(1, 0, 2, 3)
        .reshape(channels, half_rows, slab)
    )
    first = contract("sia,cij->scaj", both_sub, grid_rows)
    twist_cosine, twist_sine = twist_tables(my_freqs, my_columns, length_all)
    spread = jnp.stack(
        [
            first[0] * twist_cosine - first[1] * twist_sine,
            -first[1] * twist_cosine - first[0] * twist_sine,
        ]
    ).astype(jnp.bfloat16)

    outgoing = spread.reshape(2, channels, group, freq_rows, slab).transpose(2, 0, 1, 3, 4)
    arrived = exchange(outgoing.reshape(group, -1, 128), "ctx", False, 1)
    block = (
        arrived.reshape(group, 2, channels, freq_rows, slab)
        .transpose(1, 2, 3, 0, 4)
        .reshape(2, channels, freq_rows, block_order)
    )
    freq = contract("rcaj,sjb->srcab", block, both_full)
    freq_real = freq[0, 0] + freq[1, 1]
    freq_imag = freq[0, 1] - freq[1, 0]
    resp_real = spectrum[0].astype(jnp.float32)
    resp_imag = spectrum[1].astype(jnp.float32)
    shaped = jnp.stack(
        [
            freq_real * resp_real - freq_imag * resp_imag,
            freq_real * resp_imag + freq_imag * resp_real,
        ]
    ).astype(jnp.bfloat16)
    inner = contract("rcab,sbj->srcaj", shaped, both_full)
    inner_real = inner[0, 0] - inner[1, 1]
    inner_imag = inner[0, 1] + inner[1, 0]
    twist_cosine, twist_sine = twist_tables(local_ticks, positions, length_all)
    back = jnp.stack(
        [
            inner_real * twist_cosine - inner_imag * twist_sine,
            inner_imag * twist_cosine + inner_real * twist_sine,
        ]
    ).astype(jnp.bfloat16)

    back = lax.optimization_barrier(back)
    outgoing = back.reshape(2, channels, freq_rows, group, slab).transpose(3, 0, 1, 2, 4)
    arrived = exchange(outgoing.reshape(group, -1, 128), "ctx", False, 2)
    columns = (
        arrived.reshape(group, 2, channels, freq_rows, slab)
        .transpose(1, 2, 0, 3, 4)
        .reshape(2, channels, half_freqs, slab)
    )
    parts = contract("sia,rcaj->srcij", both_sub, columns)
    partial = ((parts[0, 0] - parts[1, 1]) * (1.0 / length_all)).astype(jnp.bfloat16)

    outgoing = partial.reshape(channels, ctx_count, rows_here, slab).transpose(1, 0, 2, 3)
    arrived = exchange(outgoing.reshape(ctx_count, channels, -1), "ctx", False, 3)
    convolved = (
        arrived.reshape(halves, group, channels, rows_here, slab)
        .astype(jnp.float32)
        .sum(0)
        .transpose(1, 2, 0, 3)
        .reshape(channels, tokens)
        .astype(jnp.bfloat16)
    )
    gated_rows = (
        q_feature.astype(jnp.float32)
        * (convolved.astype(jnp.float32) + skip_gain[:, None] * product.astype(jnp.float32))
    ).astype(jnp.bfloat16)
    gated_all = exchange(gated_rows, "tp", True, 4).reshape(tp_count * channels, tokens)
    outs_here = out_weight.shape[1] // tp_count
    tp_index = lax.axis_index("tp")
    my_weight = lax.dynamic_slice_in_dim(out_weight, tp_index * outs_here, outs_here, 1)
    return jnp.dot(my_weight.T, gated_all, preferred_element_type=jnp.float32).astype(jnp.bfloat16)


def solution(mesh):
    placed = (
        P("tp", "ctx"),
        P("tp", "ctx"),
        P("tp", "ctx"),
        P(None, "tp", "ctx", None),
        P("tp"),
        P(),
    )
    return jax.shard_map(
        local, mesh=mesh, in_specs=placed, out_specs=P("tp", "ctx"), check_vma=False
    )
```

```python
import functools
import math

import jax
import jax.numpy as jnp
from jax import lax
from jax.experimental import pallas as pl
from jax.experimental.pallas import tpu as pltpu
from jax.sharding import PartitionSpec as P

MESH = pl.DeviceIdType.MESH


def _exchange_kernel(axis, gather, x_ref, y_ref, land, send_sem, recv_sem, local_sem):
    count = land.shape[0]
    me = lax.rem(lax.axis_index(axis), count)
    base = lax.axis_index(axis) - me
    barrier = pltpu.get_barrier_semaphore()

    def greet(step, carry):
        peer = lax.rem(me + step, count)
        pl.semaphore_signal(barrier, 1, device_id={axis: base + peer}, device_id_type=MESH)
        return carry

    lax.fori_loop(1, count, greet, 0)
    pl.semaphore_wait(barrier, count - 1)

    def piece(peer):
        return x_ref if gather else x_ref.at[lax.rem(peer, x_ref.shape[0])]

    def outgoing(peer):
        return pltpu.make_async_remote_copy(
            src_ref=piece(peer), dst_ref=land.at[me], send_sem=send_sem.at[peer],
            recv_sem=recv_sem.at[me], device_id={axis: base + peer}, device_id_type=MESH)

    def incoming(source):
        return pltpu.make_async_remote_copy(
            src_ref=piece(source), dst_ref=land.at[source], send_sem=send_sem.at[source],
            recv_sem=recv_sem.at[source], device_id={axis: base + source}, device_id_type=MESH)

    def send(step, carry):
        outgoing(lax.rem(me + step, count)).start()
        return carry

    lax.fori_loop(1, count, send, 0)
    local = pltpu.make_async_copy(piece(me), land.at[me], local_sem)
    local.start()

    def finish(step, carry):
        outgoing(lax.rem(me + step, count)).wait_send()
        incoming(lax.rem(me + count - step, count)).wait_recv()
        return carry

    lax.fori_loop(1, count, finish, 0)
    local.wait()
    y_ref[...] = land[...]


def exchange(x, axis, gather, collective, count=None):
    count = count or (lax.axis_size(axis) if gather else x.shape[0])
    chunk = x.shape if gather else x.shape[1:]
    full = (count,) + tuple(chunk)
    return pl.pallas_call(
        functools.partial(_exchange_kernel, axis, gather),
        out_shape=jax.ShapeDtypeStruct(full, x.dtype),
        in_specs=[pl.BlockSpec(memory_space=pltpu.VMEM)],
        out_specs=pl.BlockSpec(memory_space=pltpu.VMEM),
        scratch_shapes=[
            pltpu.VMEM(full, x.dtype),
            pltpu.SemaphoreType.DMA((count,)),
            pltpu.SemaphoreType.DMA((count,)),
            pltpu.SemaphoreType.DMA,
        ],
        compiler_params=pltpu.CompilerParams(collective_id=collective, has_side_effects=True),
    )(x)


def fourier_tables(length_all):
    split = 1 << (int(math.log2(length_all)) // 2)
    rows_hi = length_all // split
    scale = 2.0 * math.pi / length_all
    columns = jnp.arange(length_all, dtype=jnp.int32)
    low = jnp.arange(split, dtype=jnp.int32)
    high = jnp.arange(rows_hi, dtype=jnp.int32)
    angle_low = (low[:, None] * columns[None, :] % length_all).astype(jnp.float32) * scale
    angle_high = (split * high[:, None] * columns[None, :] % length_all).astype(jnp.float32) * scale
    cos_low, sin_low = jnp.cos(angle_low)[None], jnp.sin(angle_low)[None]
    cos_high, sin_high = jnp.cos(angle_high)[:, None], jnp.sin(angle_high)[:, None]
    cosine = (cos_high * cos_low - sin_high * sin_low).reshape(length_all, length_all)
    sine = (sin_high * cos_low + cos_high * sin_low).reshape(length_all, length_all)
    return lax.optimization_barrier((cosine.astype(jnp.bfloat16), sine.astype(jnp.bfloat16)))


def twist_tables(left_index, right_index, length_all):
    phase_index = left_index[:, None] * right_index[None, :] % length_all
    angles = phase_index.astype(jnp.float32) * (2.0 * math.pi / length_all)
    return (jnp.cos(angles), jnp.sin(angles))


def contract(form, left, right):
    return jnp.einsum(form, left, right, preferred_element_type=jnp.float32)


def local(k_feature, v_feature, q_feature, spectrum, skip_gain, out_weight):
    channels, tokens = k_feature.shape
    block_order = spectrum.shape[3]
    length_all = block_order * block_order
    ctx_count = lax.axis_size("ctx")
    tp_count = lax.axis_size("tp")
    halves = 2
    group = ctx_count // halves
    slab = block_order // group
    freq_rows = block_order // ctx_count
    half_freqs = block_order // halves
    rows_here = tokens // block_order
    half_rows = block_order // 2
    ctx_index = lax.axis_index("ctx")
    half_index = ctx_index // group
    group_index = ctx_index - half_index * group
    product = (k_feature.astype(jnp.float32) * v_feature.astype(jnp.float32)).astype(jnp.bfloat16)
    cosine_full, sine_full = fourier_tables(block_order)
    both_full = jnp.stack([cosine_full, sine_full])
    both_sub = lax.dynamic_slice_in_dim(both_full, half_index * half_freqs, half_freqs, 1)[:, :, :half_rows]
    my_freqs = half_index * half_freqs + jnp.arange(half_freqs, dtype=jnp.int32)
    my_columns = group_index * slab + jnp.arange(slab, dtype=jnp.int32)
    local_ticks = ctx_index * freq_rows + jnp.arange(freq_rows, dtype=jnp.int32)
    positions = jnp.arange(block_order, dtype=jnp.int32)

    outgoing = product.reshape(channels, rows_here, group, slab).transpose(2, 0, 1, 3)
    arrived = exchange(outgoing.reshape(group, channels, -1), "ctx", False, 0, ctx_count)
    grid_rows = (
        arrived.reshape(ctx_count, channels, rows_here, slab)
        .transpose(1, 0, 2, 3)
        .reshape(channels, half_rows, slab)
    )
    first = contract("sai,cij->scaj", both_sub, grid_rows)
    twist_cosine, twist_sine = twist_tables(my_freqs, my_columns, length_all)
    spread = jnp.stack(
        [
            first[0] * twist_cosine - first[1] * twist_sine,
            -first[1] * twist_cosine - first[0] * twist_sine,
        ]
    ).astype(jnp.bfloat16)

    outgoing = spread.reshape(2, channels, group, freq_rows, slab).transpose(2, 0, 1, 3, 4)
    arrived = exchange(outgoing.reshape(group, -1, 128), "ctx", False, 1)
    block = (
        arrived.reshape(group, 2, channels, freq_rows, slab)
        .transpose(1, 2, 3, 0, 4)
        .reshape(2, channels, freq_rows, block_order)
    )
    freq = contract("rcaj,sjb->srcab", block, both_full)
    freq_real = freq[0, 0] + freq[1, 1]
    freq_imag = freq[0, 1] - freq[1, 0]
    resp_real = spectrum[0].astype(jnp.float32)
    resp_imag = spectrum[1].astype(jnp.float32)
    shaped = jnp.stack(
        [
            freq_real * resp_real - freq_imag * resp_imag,
            freq_real * resp_imag + freq_imag * resp_real,
        ]
    ).astype(jnp.bfloat16)
    inner = contract("rcab,sbj->srcaj", shaped, both_full)
    inner_real = inner[0, 0] - inner[1, 1]
    inner_imag = inner[0, 1] + inner[1, 0]
    twist_cosine, twist_sine = twist_tables(local_ticks, positions, length_all)
    back = jnp.stack(
        [
            inner_real * twist_cosine - inner_imag * twist_sine,
            inner_imag * twist_cosine + inner_real * twist_sine,
        ]
    ).astype(jnp.bfloat16)

    back = lax.optimization_barrier(back)
    outgoing = back.reshape(2, channels, freq_rows, group, slab).transpose(3, 0, 1, 2, 4)
    arrived = exchange(outgoing.reshape(group, -1, 128), "ctx", False, 2)
    columns = (
        arrived.reshape(group, 2, channels, freq_rows, slab)
        .transpose(1, 2, 0, 3, 4)
        .reshape(2, channels, half_freqs, slab)
    )
    parts = contract("sai,rcaj->srcij", both_sub, columns)
    partial = ((parts[0, 0] - parts[1, 1]) * (1.0 / length_all)).astype(jnp.bfloat16)

    outgoing = partial.reshape(channels, ctx_count, rows_here, slab).transpose(1, 0, 2, 3)
    arrived = exchange(outgoing.reshape(ctx_count, channels, -1), "ctx", False, 3)
    convolved = (
        arrived.reshape(halves, group, channels, rows_here, slab)
        .astype(jnp.float32)
        .sum(0)
        .transpose(1, 2, 0, 3)
        .reshape(channels, tokens)
        .astype(jnp.bfloat16)
    )
    gated_rows = (
        q_feature.astype(jnp.float32)
        * (convolved.astype(jnp.float32) + skip_gain[:, None] * product.astype(jnp.float32))
    ).astype(jnp.bfloat16)
    gated_all = exchange(gated_rows, "tp", True, 4).reshape(tp_count * channels, tokens)
    outs_here = out_weight.shape[1] // tp_count
    tp_index = lax.axis_index("tp")
    my_weight = lax.dynamic_slice_in_dim(out_weight, tp_index * outs_here, outs_here, 1)
    return jnp.dot(my_weight.T, gated_all, preferred_element_type=jnp.float32).astype(jnp.bfloat16)


def solution(mesh):
    placed = (
        P("tp", "ctx"),
        P("tp", "ctx"),
        P("tp", "ctx"),
        P(None, "tp", "ctx", None),
        P("tp"),
        P(),
    )
    return jax.shard_map(
        local, mesh=mesh, in_specs=placed, out_specs=P("tp", "ctx"), check_vma=False
    )
```

```python
import functools
import math

import jax
import jax.numpy as jnp
from jax import lax
from jax.experimental import pallas as pl
from jax.experimental.pallas import tpu as pltpu
from jax.sharding import PartitionSpec as P

MESH = pl.DeviceIdType.MESH


def _exchange_kernel(axis, gather, x_ref, y_ref, land, send_sem, recv_sem, local_sem):
    count = land.shape[0]
    me = lax.rem(lax.axis_index(axis), count)
    base = lax.axis_index(axis) - me
    barrier = pltpu.get_barrier_semaphore()

    def greet(step, carry):
        peer = lax.rem(me + step, count)
        pl.semaphore_signal(barrier, 1, device_id={axis: base + peer}, device_id_type=MESH)
        return carry

    lax.fori_loop(1, count, greet, 0)
    pl.semaphore_wait(barrier, count - 1)

    def piece(peer):
        return x_ref if gather else x_ref.at[lax.rem(peer, x_ref.shape[0])]

    def outgoing(peer):
        return pltpu.make_async_remote_copy(
            src_ref=piece(peer), dst_ref=land.at[me], send_sem=send_sem.at[peer],
            recv_sem=recv_sem.at[me], device_id={axis: base + peer}, device_id_type=MESH)

    def incoming(source):
        return pltpu.make_async_remote_copy(
            src_ref=piece(source), dst_ref=land.at[source], send_sem=send_sem.at[source],
            recv_sem=recv_sem.at[source], device_id={axis: base + source}, device_id_type=MESH)

    def send(step, carry):
        outgoing(lax.rem(me + step, count)).start()
        return carry

    lax.fori_loop(1, count, send, 0)
    local = pltpu.make_async_copy(piece(me), land.at[me], local_sem)
    local.start()

    def finish(step, carry):
        outgoing(lax.rem(me + step, count)).wait_send()
        incoming(lax.rem(me + count - step, count)).wait_recv()
        return carry

    lax.fori_loop(1, count, finish, 0)
    local.wait()
    y_ref[...] = land[...]


def exchange(x, axis, gather, collective, count=None):
    count = count or (lax.axis_size(axis) if gather else x.shape[0])
    chunk = x.shape if gather else x.shape[1:]
    full = (count,) + tuple(chunk)
    return pl.pallas_call(
        functools.partial(_exchange_kernel, axis, gather),
        out_shape=jax.ShapeDtypeStruct(full, x.dtype),
        in_specs=[pl.BlockSpec(memory_space=pltpu.VMEM)],
        out_specs=pl.BlockSpec(memory_space=pltpu.VMEM),
        scratch_shapes=[
            pltpu.VMEM(full, x.dtype),
            pltpu.SemaphoreType.DMA((count,)),
            pltpu.SemaphoreType.DMA((count,)),
            pltpu.SemaphoreType.DMA,
        ],
        compiler_params=pltpu.CompilerParams(collective_id=collective, has_side_effects=True),
    )(x)


def fourier_tables(length_all):
    split = 1 << (int(math.log2(length_all)) // 2)
    rows_hi = length_all // split
    scale = 2.0 * math.pi / length_all
    columns = jnp.arange(length_all, dtype=jnp.int32)
    low = jnp.arange(split, dtype=jnp.int32)
    high = jnp.arange(rows_hi, dtype=jnp.int32)
    angle_low = (low[:, None] * columns[None, :] % length_all).astype(jnp.float32) * scale
    angle_high = (split * high[:, None] * columns[None, :] % length_all).astype(jnp.float32) * scale
    cos_low, sin_low = jnp.cos(angle_low)[None], jnp.sin(angle_low)[None]
    cos_high, sin_high = jnp.cos(angle_high)[:, None], jnp.sin(angle_high)[:, None]
    cosine = (cos_high * cos_low - sin_high * sin_low).reshape(length_all, length_all)
    sine = (sin_high * cos_low + cos_high * sin_low).reshape(length_all, length_all)
    return lax.optimization_barrier((cosine.astype(jnp.bfloat16), sine.astype(jnp.bfloat16)))


def twist_tables(left_index, right_index, length_all):
    phase_index = left_index[:, None] * right_index[None, :] % length_all
    angles = phase_index.astype(jnp.float32) * (2.0 * math.pi / length_all)
    return (jnp.cos(angles), jnp.sin(angles))


def contract(form, left, right):
    return jnp.einsum(form, left, right, preferred_element_type=jnp.float32)


def local(k_feature, v_feature, q_feature, spectrum, skip_gain, out_weight):
    channels, tokens = k_feature.shape
    block_order = spectrum.shape[3]
    length_all = block_order * block_order
    ctx_count = lax.axis_size("ctx")
    tp_count = lax.axis_size("tp")
    halves = 2
    group = ctx_count // halves
    slab = block_order // group
    freq_rows = block_order // ctx_count
    lanes = channels * freq_rows
    half_freqs = block_order // halves
    rows_here = tokens // block_order
    half_rows = block_order // 2
    ctx_index = lax.axis_index("ctx")
    half_index = ctx_index // group
    group_index = ctx_index - half_index * group
    product = (k_feature.astype(jnp.float32) * v_feature.astype(jnp.float32)).astype(jnp.bfloat16)
    cosine_full, sine_full = fourier_tables(block_order)
    both_full = jnp.stack([cosine_full, sine_full])
    both_sub = lax.dynamic_slice_in_dim(both_full, half_index * half_freqs, half_freqs, 1)[:, :, :half_rows]
    my_freqs = half_index * half_freqs + jnp.arange(half_freqs, dtype=jnp.int32)
    my_columns = group_index * slab + jnp.arange(slab, dtype=jnp.int32)
    local_ticks = ctx_index * freq_rows + jnp.arange(freq_rows, dtype=jnp.int32)
    positions = jnp.arange(block_order, dtype=jnp.int32)

    outgoing = product.reshape(channels, rows_here, group, slab).transpose(2, 0, 1, 3)
    arrived = exchange(outgoing.reshape(group, channels, -1), "ctx", False, 0, ctx_count)
    grid_rows = (
        arrived.reshape(ctx_count, channels, rows_here, slab)
        .transpose(1, 0, 2, 3)
        .reshape(channels, half_rows, slab)
    )
    first = contract("sai,cij->scaj", both_sub, grid_rows)
    twist_cosine, twist_sine = twist_tables(my_freqs, my_columns, length_all)
    spread = jnp.stack(
        [
            first[0] * twist_cosine - first[1] * twist_sine,
            -first[1] * twist_cosine - first[0] * twist_sine,
        ]
    ).astype(jnp.bfloat16)

    outgoing = spread.reshape(2, channels, group, freq_rows, slab).transpose(2, 0, 1, 3, 4)
    arrived = exchange(outgoing.reshape(group, -1, 128), "ctx", False, 1)
    block = (
        arrived.reshape(group, 2, channels, freq_rows, slab)
        .transpose(1, 2, 3, 0, 4)
        .reshape(2, channels, freq_rows, block_order)
    )
    freq = contract("rcaj,sjb->srcab", block, both_full)
    freq_real = freq[0, 0] + freq[1, 1]
    freq_imag = freq[0, 1] - freq[1, 0]
    resp_real = spectrum[0].astype(jnp.float32)
    resp_imag = spectrum[1].astype(jnp.float32)
    shaped = jnp.stack(
        [
            freq_real * resp_real - freq_imag * resp_imag,
            freq_real * resp_imag + freq_imag * resp_real,
        ]
    ).astype(jnp.bfloat16)
    inner = contract("sjb,kb->sjk", both_full, shaped.reshape(2 * lanes, block_order))
    inner_real = inner[0, :, :lanes] - inner[1, :, lanes:]
    inner_imag = inner[0, :, lanes:] + inner[1, :, :lanes]
    twist_cosine, twist_sine = twist_tables(positions, local_ticks, length_all)
    twist_cosine = jnp.tile(twist_cosine, (1, channels))
    twist_sine = jnp.tile(twist_sine, (1, channels))
    back = jnp.concatenate(
        [
            inner_real * twist_cosine - inner_imag * twist_sine,
            inner_imag * twist_cosine + inner_real * twist_sine,
        ],
        axis=1,
    ).astype(jnp.bfloat16)

    arrived = exchange(back.reshape(group, slab, 2 * lanes), "ctx", False, 2)
    columns = (
        arrived.reshape(group, slab, 2, channels, freq_rows)
        .transpose(2, 3, 0, 4, 1)
        .reshape(2, channels, half_freqs, slab)
    )
    parts = contract("sai,rcaj->srcij", both_sub, columns)
    partial = ((parts[0, 0] - parts[1, 1]) * (1.0 / length_all)).astype(jnp.bfloat16)

    outgoing = partial.reshape(channels, ctx_count, rows_here, slab).transpose(1, 0, 2, 3)
    arrived = exchange(outgoing.reshape(ctx_count, channels, -1), "ctx", False, 3)
    convolved = (
        arrived.reshape(halves, group, channels, rows_here, slab)
        .astype(jnp.float32)
        .sum(0)
        .transpose(1, 2, 0, 3)
        .reshape(channels, tokens)
        .astype(jnp.bfloat16)
    )
    gated_rows = (
        q_feature.astype(jnp.float32)
        * (convolved.astype(jnp.float32) + skip_gain[:, None] * product.astype(jnp.float32))
    ).astype(jnp.bfloat16)
    gated_all = exchange(gated_rows, "tp", True, 4).reshape(tp_count * channels, tokens)
    outs_here = out_weight.shape[1] // tp_count
    tp_index = lax.axis_index("tp")
    my_weight = lax.dynamic_slice_in_dim(out_weight, tp_index * outs_here, outs_here, 1)
    return jnp.dot(my_weight.T, gated_all, preferred_element_type=jnp.float32).astype(jnp.bfloat16)


def solution(mesh):
    placed = (
        P("tp", "ctx"),
        P("tp", "ctx"),
        P("tp", "ctx"),
        P(None, "tp", "ctx", None),
        P("tp"),
        P(),
    )
    return jax.shard_map(
        local, mesh=mesh, in_specs=placed, out_specs=P("tp", "ctx"), check_vma=False
    )
```

```python
import functools
import math

import jax
import jax.numpy as jnp
from jax import lax
from jax.experimental import pallas as pl
from jax.experimental.pallas import tpu as pltpu
from jax.sharding import PartitionSpec as P

MESH = pl.DeviceIdType.MESH


def _exchange_kernel(axis, gather, x_ref, y_ref, land, send_sem, recv_sem, local_sem):
    count = land.shape[0]
    me = lax.rem(lax.axis_index(axis), count)
    base = lax.axis_index(axis) - me
    barrier = pltpu.get_barrier_semaphore()

    def greet(step, carry):
        peer = lax.rem(me + step, count)
        pl.semaphore_signal(barrier, 1, device_id={axis: base + peer}, device_id_type=MESH)
        return carry

    lax.fori_loop(1, count, greet, 0)
    pl.semaphore_wait(barrier, count - 1)

    def piece(peer):
        return x_ref if gather else x_ref.at[lax.rem(peer, x_ref.shape[0])]

    def outgoing(peer):
        return pltpu.make_async_remote_copy(
            src_ref=piece(peer), dst_ref=land.at[me], send_sem=send_sem.at[peer],
            recv_sem=recv_sem.at[me], device_id={axis: base + peer}, device_id_type=MESH)

    def incoming(source):
        return pltpu.make_async_remote_copy(
            src_ref=piece(source), dst_ref=land.at[source], send_sem=send_sem.at[source],
            recv_sem=recv_sem.at[source], device_id={axis: base + source}, device_id_type=MESH)

    def send(step, carry):
        outgoing(lax.rem(me + step, count)).start()
        return carry

    lax.fori_loop(1, count, send, 0)
    local = pltpu.make_async_copy(piece(me), land.at[me], local_sem)
    local.start()

    def finish(step, carry):
        outgoing(lax.rem(me + step, count)).wait_send()
        incoming(lax.rem(me + count - step, count)).wait_recv()
        return carry

    lax.fori_loop(1, count, finish, 0)
    local.wait()
    y_ref[...] = land[...]


def exchange(x, axis, gather, collective, count=None):
    count = count or (lax.axis_size(axis) if gather else x.shape[0])
    chunk = x.shape if gather else x.shape[1:]
    full = (count,) + tuple(chunk)
    return pl.pallas_call(
        functools.partial(_exchange_kernel, axis, gather),
        out_shape=jax.ShapeDtypeStruct(full, x.dtype),
        in_specs=[pl.BlockSpec(memory_space=pltpu.VMEM)],
        out_specs=pl.BlockSpec(memory_space=pltpu.VMEM),
        scratch_shapes=[
            pltpu.VMEM(full, x.dtype),
            pltpu.SemaphoreType.DMA((count,)),
            pltpu.SemaphoreType.DMA((count,)),
            pltpu.SemaphoreType.DMA,
        ],
        compiler_params=pltpu.CompilerParams(collective_id=collective, has_side_effects=True),
    )(x)


def fourier_tables(length_all):
    split = 1 << (int(math.log2(length_all)) // 2)
    rows_hi = length_all // split
    scale = 2.0 * math.pi / length_all
    columns = jnp.arange(length_all, dtype=jnp.int32)
    low = jnp.arange(split, dtype=jnp.int32)
    high = jnp.arange(rows_hi, dtype=jnp.int32)
    angle_low = (low[:, None] * columns[None, :] % length_all).astype(jnp.float32) * scale
    angle_high = (split * high[:, None] * columns[None, :] % length_all).astype(jnp.float32) * scale
    cos_low, sin_low = jnp.cos(angle_low)[None], jnp.sin(angle_low)[None]
    cos_high, sin_high = jnp.cos(angle_high)[:, None], jnp.sin(angle_high)[:, None]
    cosine = (cos_high * cos_low - sin_high * sin_low).reshape(length_all, length_all)
    sine = (sin_high * cos_low + cos_high * sin_low).reshape(length_all, length_all)
    return lax.optimization_barrier((cosine.astype(jnp.bfloat16), sine.astype(jnp.bfloat16)))


def twist_tables(left_index, right_index, length_all):
    phase_index = left_index[:, None] * right_index[None, :] % length_all
    angles = phase_index.astype(jnp.float32) * (2.0 * math.pi / length_all)
    return (jnp.cos(angles), jnp.sin(angles))


def contract(form, left, right):
    return jnp.einsum(form, left, right, preferred_element_type=jnp.float32)


def local(k_feature, v_feature, q_feature, spectrum, skip_gain, out_weight):
    channels, tokens = k_feature.shape
    block_order = spectrum.shape[3]
    length_all = block_order * block_order
    ctx_count = lax.axis_size("ctx")
    tp_count = lax.axis_size("tp")
    halves = 2
    group = ctx_count // halves
    slab = block_order // group
    freq_rows = block_order // ctx_count
    half_freqs = block_order // halves
    rows_here = tokens // block_order
    half_rows = block_order // 2
    ctx_index = lax.axis_index("ctx")
    half_index = ctx_index // group
    group_index = ctx_index - half_index * group
    product = (k_feature.astype(jnp.float32) * v_feature.astype(jnp.float32)).astype(jnp.bfloat16)
    cosine_full, sine_full = fourier_tables(block_order)
    both_full = jnp.stack([cosine_full, sine_full])
    both_sub = lax.dynamic_slice_in_dim(both_full, half_index * half_freqs, half_freqs, 1)[:, :, :half_rows]
    my_freqs = half_index * half_freqs + jnp.arange(half_freqs, dtype=jnp.int32)
    my_columns = group_index * slab + jnp.arange(slab, dtype=jnp.int32)
    local_ticks = ctx_index * freq_rows + jnp.arange(freq_rows, dtype=jnp.int32)
    positions = jnp.arange(block_order, dtype=jnp.int32)

    outgoing = product.reshape(channels, rows_here, group, slab).transpose(2, 0, 1, 3)
    arrived = exchange(outgoing.reshape(group, channels, -1), "ctx", False, 0, ctx_count)
    grid_rows = (
        arrived.reshape(ctx_count, channels, rows_here, slab)
        .transpose(1, 0, 2, 3)
        .reshape(channels, half_rows, slab)
    )
    first = contract("sai,cij->scaj", both_sub, grid_rows)
    twist_cosine, twist_sine = twist_tables(my_freqs, my_columns, length_all)
    spread = jnp.stack(
        [
            first[0] * twist_cosine - first[1] * twist_sine,
            -first[1] * twist_cosine - first[0] * twist_sine,
        ]
    ).astype(jnp.bfloat16)

    outgoing = spread.reshape(2, channels, group, freq_rows, slab).transpose(2, 0, 1, 3, 4)
    arrived = exchange(outgoing.reshape(group, -1, 128), "ctx", False, 1)
    block = (
        arrived.reshape(group, 2, channels, freq_rows, slab)
        .transpose(1, 2, 3, 0, 4)
        .reshape(2, channels, freq_rows, block_order)
    )
    freq = contract("rcaj,sjb->srcab", block, both_full)
    freq_real = freq[0, 0] + freq[1, 1]
    freq_imag = freq[0, 1] - freq[1, 0]
    resp_real = spectrum[0].astype(jnp.float32)
    resp_imag = spectrum[1].astype(jnp.float32)
    shaped = jnp.stack(
        [
            freq_real * resp_real - freq_imag * resp_imag,
            freq_real * resp_imag + freq_imag * resp_real,
        ]
    ).astype(jnp.bfloat16)
    inner = contract("rcab,sbj->srcaj", shaped, both_full)
    inner_real = inner[0, 0] - inner[1, 1]
    inner_imag = inner[0, 1] + inner[1, 0]
    twist_cosine, twist_sine = twist_tables(local_ticks, positions, length_all)
    back = jnp.stack(
        [
            inner_real * twist_cosine - inner_imag * twist_sine,
            inner_imag * twist_cosine + inner_real * twist_sine,
        ]
    ).astype(jnp.bfloat16)

    back = lax.optimization_barrier(back)
    outgoing = back.reshape(2, channels, freq_rows, group, slab).transpose(3, 0, 1, 2, 4)
    arrived = exchange(outgoing.reshape(group, -1, 128), "ctx", False, 2)
    columns = (
        arrived.reshape(group, 2, channels, freq_rows, slab)
        .transpose(1, 2, 0, 3, 4)
        .reshape(2, channels, half_freqs, slab)
    )
    parts = contract("sai,rcaj->srcij", both_sub, columns)
    partial = ((parts[0, 0] - parts[1, 1]) * (1.0 / length_all)).astype(jnp.bfloat16)

    outgoing = partial.reshape(channels, ctx_count, rows_here, slab).transpose(1, 0, 2, 3)
    arrived = exchange(outgoing.reshape(ctx_count, channels, -1), "ctx", False, 3)
    convolved = (
        arrived.reshape(halves, group, channels, rows_here, slab)
        .astype(jnp.float32)
        .sum(0)
        .transpose(1, 2, 0, 3)
        .reshape(channels, tokens)
        .astype(jnp.bfloat16)
    )
    gated_rows = (
        q_feature.astype(jnp.float32)
        * (convolved.astype(jnp.float32) + skip_gain[:, None] * product.astype(jnp.float32))
    ).astype(jnp.bfloat16)
    token_block = tokens // tp_count
    outgoing = gated_rows.reshape(channels, tp_count, token_block).transpose(1, 0, 2)
    arrived = exchange(outgoing, "tp", False, 4)
    block_mixed = jnp.dot(
        out_weight.T, arrived.reshape(tp_count * channels, token_block), preferred_element_type=jnp.float32
    ).astype(jnp.bfloat16)
    outs_here = out_weight.shape[1] // tp_count
    returned = exchange(block_mixed.reshape(tp_count, outs_here, token_block), "tp", False, 5)
    return returned.transpose(1, 0, 2).reshape(outs_here, tokens)


def solution(mesh):
    placed = (
        P("tp", "ctx"),
        P("tp", "ctx"),
        P("tp", "ctx"),
        P(None, "tp", "ctx", None),
        P("tp"),
        P(),
    )
    return jax.shard_map(
        local, mesh=mesh, in_specs=placed, out_specs=P("tp", "ctx"), check_vma=False
    )
```

```python
import functools
import math

import jax
import jax.numpy as jnp
from jax import lax
from jax.experimental import pallas as pl
from jax.experimental.pallas import tpu as pltpu
from jax.sharding import PartitionSpec as P

MESH = pl.DeviceIdType.MESH


def _exchange_kernel(axis, gather, x_ref, y_ref, land, send_sem, recv_sem, local_sem):
    count = land.shape[0]
    me = lax.rem(lax.axis_index(axis), count)
    base = lax.axis_index(axis) - me
    barrier = pltpu.get_barrier_semaphore()

    def greet(step, carry):
        peer = lax.rem(me + step, count)
        pl.semaphore_signal(barrier, 1, device_id={axis: base + peer}, device_id_type=MESH)
        return carry

    lax.fori_loop(1, count, greet, 0)
    pl.semaphore_wait(barrier, count - 1)

    def piece(peer):
        return x_ref if gather else x_ref.at[lax.rem(peer, x_ref.shape[0])]

    def outgoing(peer):
        return pltpu.make_async_remote_copy(
            src_ref=piece(peer), dst_ref=land.at[me], send_sem=send_sem.at[peer],
            recv_sem=recv_sem.at[me], device_id={axis: base + peer}, device_id_type=MESH)

    def incoming(source):
        return pltpu.make_async_remote_copy(
            src_ref=piece(source), dst_ref=land.at[source], send_sem=send_sem.at[source],
            recv_sem=recv_sem.at[source], device_id={axis: base + source}, device_id_type=MESH)

    def send(step, carry):
        outgoing(lax.rem(me + step, count)).start()
        return carry

    lax.fori_loop(1, count, send, 0)
    local = pltpu.make_async_copy(piece(me), land.at[me], local_sem)
    local.start()

    def finish(step, carry):
        outgoing(lax.rem(me + step, count)).wait_send()
        incoming(lax.rem(me + count - step, count)).wait_recv()
        return carry

    lax.fori_loop(1, count, finish, 0)
    local.wait()
    y_ref[...] = land[...]


def exchange(x, axis, gather, collective, count=None):
    count = count or (lax.axis_size(axis) if gather else x.shape[0])
    chunk = x.shape if gather else x.shape[1:]
    full = (count,) + tuple(chunk)
    return pl.pallas_call(
        functools.partial(_exchange_kernel, axis, gather),
        out_shape=jax.ShapeDtypeStruct(full, x.dtype),
        in_specs=[pl.BlockSpec(memory_space=pltpu.VMEM)],
        out_specs=pl.BlockSpec(memory_space=pltpu.VMEM),
        scratch_shapes=[
            pltpu.VMEM(full, x.dtype),
            pltpu.SemaphoreType.DMA((count,)),
            pltpu.SemaphoreType.DMA((count,)),
            pltpu.SemaphoreType.DMA,
        ],
        compiler_params=pltpu.CompilerParams(collective_id=collective, has_side_effects=True),
    )(x)


def _projection_kernel(x_ref, w_ref, y_ref, land, mixed, back, send_a, recv_a, send_b, recv_b, own):
    count, channels = land.shape[0], land.shape[1]
    outs_here = mixed.shape[1]
    me = lax.axis_index("tp")
    barrier = pltpu.get_barrier_semaphore()

    def greet(step, carry):
        pl.semaphore_signal(barrier, 1, device_id={"tp": lax.rem(me + step, count)}, device_id_type=MESH)
        return carry

    lax.fori_loop(1, count, greet, 0)
    pl.semaphore_wait(barrier, count - 1)

    def there(src, dst, sends, recvs, peer, slot):
        return pltpu.make_async_remote_copy(
            src_ref=src.at[peer], dst_ref=dst.at[slot], send_sem=sends.at[peer],
            recv_sem=recvs.at[slot], device_id={"tp": peer}, device_id_type=MESH)

    def trade(src, dst, sends, recvs, flag):
        def send(step, carry):
            there(src, dst, sends, recvs, lax.rem(me + step, count), me).start()
            return carry

        lax.fori_loop(1, count, send, 0)
        local = pltpu.make_async_copy(src.at[me], dst.at[me], own.at[flag])
        local.start()

        def finish(step, carry):
            there(src, dst, sends, recvs, lax.rem(me + step, count), me).wait_send()
            source = lax.rem(me + count - step, count)
            there(src, dst, sends, recvs, source, source).wait_recv()
            return carry

        lax.fori_loop(1, count, finish, 0)
        local.wait()

    trade(x_ref, land, send_a, recv_a, 0)
    total = jnp.zeros((count * outs_here, land.shape[2]), jnp.float32)
    for group_index in range(count):
        for channel in range(channels):
            row = land[group_index, channel : channel + 1, :].astype(jnp.float32)
            total = total + w_ref[group_index * channels + channel] * row
    for group_index in range(count):
        mixed[group_index] = total[group_index * outs_here : (group_index + 1) * outs_here].astype(mixed.dtype)
    trade(mixed, back, send_b, recv_b, 1)
    y_ref[...] = back[...]


def project_over_tp(x, weight, outs_here, collective):
    count, channels, block = x.shape
    return pl.pallas_call(
        _projection_kernel,
        out_shape=jax.ShapeDtypeStruct((count, outs_here, block), x.dtype),
        in_specs=[pl.BlockSpec(memory_space=pltpu.VMEM)] * 2,
        out_specs=pl.BlockSpec(memory_space=pltpu.VMEM),
        scratch_shapes=[
            pltpu.VMEM(x.shape, x.dtype),
            pltpu.VMEM((count, outs_here, block), x.dtype),
            pltpu.VMEM((count, outs_here, block), x.dtype),
            pltpu.SemaphoreType.DMA((count,)),
            pltpu.SemaphoreType.DMA((count,)),
            pltpu.SemaphoreType.DMA((count,)),
            pltpu.SemaphoreType.DMA((count,)),
            pltpu.SemaphoreType.DMA((2,)),
        ],
        compiler_params=pltpu.CompilerParams(collective_id=collective, has_side_effects=True),
    )(x, weight)


def fourier_tables(length_all):
    split = 1 << (int(math.log2(length_all)) // 2)
    rows_hi = length_all // split
    scale = 2.0 * math.pi / length_all
    columns = jnp.arange(length_all, dtype=jnp.int32)
    low = jnp.arange(split, dtype=jnp.int32)
    high = jnp.arange(rows_hi, dtype=jnp.int32)
    angle_low = (low[:, None] * columns[None, :] % length_all).astype(jnp.float32) * scale
    angle_high = (split * high[:, None] * columns[None, :] % length_all).astype(jnp.float32) * scale
    cos_low, sin_low = jnp.cos(angle_low)[None], jnp.sin(angle_low)[None]
    cos_high, sin_high = jnp.cos(angle_high)[:, None], jnp.sin(angle_high)[:, None]
    cosine = (cos_high * cos_low - sin_high * sin_low).reshape(length_all, length_all)
    sine = (sin_high * cos_low + cos_high * sin_low).reshape(length_all, length_all)
    return lax.optimization_barrier((cosine.astype(jnp.bfloat16), sine.astype(jnp.bfloat16)))


def twist_tables(left_index, right_index, length_all):
    phase_index = left_index[:, None] * right_index[None, :] % length_all
    angles = phase_index.astype(jnp.float32) * (2.0 * math.pi / length_all)
    return (jnp.cos(angles), jnp.sin(angles))


def contract(form, left, right):
    return jnp.einsum(form, left, right, preferred_element_type=jnp.float32)


def local(k_feature, v_feature, q_feature, spectrum, skip_gain, out_weight):
    channels, tokens = k_feature.shape
    block_order = spectrum.shape[3]
    length_all = block_order * block_order
    ctx_count = lax.axis_size("ctx")
    tp_count = lax.axis_size("tp")
    halves = 2
    group = ctx_count // halves
    slab = block_order // group
    freq_rows = block_order // ctx_count
    half_freqs = block_order // halves
    rows_here = tokens // block_order
    half_rows = block_order // 2
    ctx_index = lax.axis_index("ctx")
    half_index = ctx_index // group
    group_index = ctx_index - half_index * group
    product = (k_feature.astype(jnp.float32) * v_feature.astype(jnp.float32)).astype(jnp.bfloat16)
    cosine_full, sine_full = fourier_tables(block_order)
    both_full = jnp.stack([cosine_full, sine_full])
    both_sub = lax.dynamic_slice_in_dim(both_full, half_index * half_freqs, half_freqs, 1)[:, :, :half_rows]
    my_freqs = half_index * half_freqs + jnp.arange(half_freqs, dtype=jnp.int32)
    my_columns = group_index * slab + jnp.arange(slab, dtype=jnp.int32)
    local_ticks = ctx_index * freq_rows + jnp.arange(freq_rows, dtype=jnp.int32)
    positions = jnp.arange(block_order, dtype=jnp.int32)

    outgoing = product.reshape(channels, rows_here, group, slab).transpose(2, 0, 1, 3)
    arrived = exchange(outgoing.reshape(group, channels, -1), "ctx", False, 0, ctx_count)
    grid_rows = (
        arrived.reshape(ctx_count, channels, rows_here, slab)
        .transpose(1, 0, 2, 3)
        .reshape(channels, half_rows, slab)
    )
    first = contract("sai,cij->scaj", both_sub, grid_rows)
    twist_cosine, twist_sine = twist_tables(my_freqs, my_columns, length_all)
    spread = jnp.stack(
        [
            first[0] * twist_cosine - first[1] * twist_sine,
            -first[1] * twist_cosine - first[0] * twist_sine,
        ]
    ).astype(jnp.bfloat16)

    outgoing = spread.reshape(2, channels, group, freq_rows, slab).transpose(2, 0, 1, 3, 4)
    arrived = exchange(outgoing.reshape(group, -1, 128), "ctx", False, 1)
    block = (
        arrived.reshape(group, 2, channels, freq_rows, slab)
        .transpose(1, 2, 3, 0, 4)
        .reshape(2, channels, freq_rows, block_order)
    )
    freq = contract("rcaj,sjb->srcab", block, both_full)
    freq_real = freq[0, 0] + freq[1, 1]
    freq_imag = freq[0, 1] - freq[1, 0]
    resp_real = spectrum[0].astype(jnp.float32)
    resp_imag = spectrum[1].astype(jnp.float32)
    shaped = jnp.stack(
        [
            freq_real * resp_real - freq_imag * resp_imag,
            freq_real * resp_imag + freq_imag * resp_real,
        ]
    ).astype(jnp.bfloat16)
    inner = contract("rcab,sbj->srcaj", shaped, both_full)
    inner_real = inner[0, 0] - inner[1, 1]
    inner_imag = inner[0, 1] + inner[1, 0]
    twist_cosine, twist_sine = twist_tables(local_ticks, positions, length_all)
    back = jnp.stack(
        [
            inner_real * twist_cosine - inner_imag * twist_sine,
            inner_imag * twist_cosine + inner_real * twist_sine,
        ]
    ).astype(jnp.bfloat16)

    back = lax.optimization_barrier(back)
    outgoing = back.reshape(2, channels, freq_rows, group, slab).transpose(3, 0, 1, 2, 4)
    arrived = exchange(outgoing.reshape(group, -1, 128), "ctx", False, 2)
    columns = (
        arrived.reshape(group, 2, channels, freq_rows, slab)
        .transpose(1, 2, 0, 3, 4)
        .reshape(2, channels, half_freqs, slab)
    )
    parts = contract("sai,rcaj->srcij", both_sub, columns)
    partial = ((parts[0, 0] - parts[1, 1]) * (1.0 / length_all)).astype(jnp.bfloat16)

    outgoing = partial.reshape(channels, ctx_count, rows_here, slab).transpose(1, 0, 2, 3)
    arrived = exchange(outgoing.reshape(ctx_count, channels, -1), "ctx", False, 3)
    convolved = (
        arrived.reshape(halves, group, channels, rows_here, slab)
        .astype(jnp.float32)
        .sum(0)
        .transpose(1, 2, 0, 3)
        .reshape(channels, tokens)
        .astype(jnp.bfloat16)
    )
    gated_rows = (
        q_feature.astype(jnp.float32)
        * (convolved.astype(jnp.float32) + skip_gain[:, None] * product.astype(jnp.float32))
    ).astype(jnp.bfloat16)
    token_block = tokens // tp_count
    outgoing = gated_rows.reshape(channels, tp_count, token_block).transpose(1, 0, 2)
    outs_here = out_weight.shape[1] // tp_count
    weight_columns = out_weight.astype(jnp.float32).reshape(tp_count * channels, tp_count * outs_here, 1)
    returned = project_over_tp(outgoing, weight_columns, outs_here, 4)
    return returned.transpose(1, 0, 2).reshape(outs_here, tokens)


def solution(mesh):
    placed = (
        P("tp", "ctx"),
        P("tp", "ctx"),
        P("tp", "ctx"),
        P(None, "tp", "ctx", None),
        P("tp"),
        P(),
    )
    return jax.shard_map(
        local, mesh=mesh, in_specs=placed, out_specs=P("tp", "ctx"), check_vma=False
    )
```

```python
import functools
import math

import jax
import jax.numpy as jnp
from jax import lax
from jax.experimental import pallas as pl
from jax.experimental.pallas import tpu as pltpu
from jax.sharding import PartitionSpec as P

MESH = pl.DeviceIdType.MESH


def _exchange_kernel(axis, gather, x_ref, y_ref, land, send_sem, recv_sem, local_sem):
    count = land.shape[0]
    me = lax.rem(lax.axis_index(axis), count)
    base = lax.axis_index(axis) - me
    barrier = pltpu.get_barrier_semaphore()

    def greet(step, carry):
        peer = lax.rem(me + step, count)
        pl.semaphore_signal(barrier, 1, device_id={axis: base + peer}, device_id_type=MESH)
        return carry

    lax.fori_loop(1, count, greet, 0)
    pl.semaphore_wait(barrier, count - 1)

    def piece(peer):
        return x_ref if gather else x_ref.at[lax.rem(peer, x_ref.shape[0])]

    def outgoing(peer):
        return pltpu.make_async_remote_copy(
            src_ref=piece(peer), dst_ref=land.at[me], send_sem=send_sem.at[peer],
            recv_sem=recv_sem.at[me], device_id={axis: base + peer}, device_id_type=MESH)

    def incoming(source):
        return pltpu.make_async_remote_copy(
            src_ref=piece(source), dst_ref=land.at[source], send_sem=send_sem.at[source],
            recv_sem=recv_sem.at[source], device_id={axis: base + source}, device_id_type=MESH)

    def send(step, carry):
        outgoing(lax.rem(me + step, count)).start()
        return carry

    lax.fori_loop(1, count, send, 0)
    local = pltpu.make_async_copy(piece(me), land.at[me], local_sem)
    local.start()

    def finish(step, carry):
        outgoing(lax.rem(me + step, count)).wait_send()
        incoming(lax.rem(me + count - step, count)).wait_recv()
        return carry

    lax.fori_loop(1, count, finish, 0)
    local.wait()
    y_ref[...] = land[...]


def exchange(x, axis, gather, collective, count=None):
    count = count or (lax.axis_size(axis) if gather else x.shape[0])
    chunk = x.shape if gather else x.shape[1:]
    full = (count,) + tuple(chunk)
    return pl.pallas_call(
        functools.partial(_exchange_kernel, axis, gather),
        out_shape=jax.ShapeDtypeStruct(full, x.dtype),
        in_specs=[pl.BlockSpec(memory_space=pltpu.VMEM)],
        out_specs=pl.BlockSpec(memory_space=pltpu.VMEM),
        scratch_shapes=[
            pltpu.VMEM(full, x.dtype),
            pltpu.SemaphoreType.DMA((count,)),
            pltpu.SemaphoreType.DMA((count,)),
            pltpu.SemaphoreType.DMA,
        ],
        compiler_params=pltpu.CompilerParams(collective_id=collective, has_side_effects=True),
    )(x)


def _projection_kernel(x_ref, w_ref, y_ref, land, mixed, back, send_a, recv_a, send_b, recv_b, own):
    count, channels = land.shape[0], land.shape[1]
    outs_here = mixed.shape[1]
    me = lax.axis_index("tp")
    barrier = pltpu.get_barrier_semaphore()

    def greet(step, carry):
        pl.semaphore_signal(barrier, 1, device_id={"tp": lax.rem(me + step, count)}, device_id_type=MESH)
        return carry

    lax.fori_loop(1, count, greet, 0)
    pl.semaphore_wait(barrier, count - 1)

    def there(src, dst, sends, recvs, peer, slot):
        return pltpu.make_async_remote_copy(
            src_ref=src.at[peer], dst_ref=dst.at[slot], send_sem=sends.at[peer],
            recv_sem=recvs.at[slot], device_id={"tp": peer}, device_id_type=MESH)

    def trade(src, dst, sends, recvs, flag):
        def send(step, carry):
            there(src, dst, sends, recvs, lax.rem(me + step, count), me).start()
            return carry

        lax.fori_loop(1, count, send, 0)
        local = pltpu.make_async_copy(src.at[me], dst.at[me], own.at[flag])
        local.start()

        def finish(step, carry):
            there(src, dst, sends, recvs, lax.rem(me + step, count), me).wait_send()
            source = lax.rem(me + count - step, count)
            there(src, dst, sends, recvs, source, source).wait_recv()
            return carry

        lax.fori_loop(1, count, finish, 0)
        local.wait()

    trade(x_ref, land, send_a, recv_a, 0)
    total = jnp.zeros((count * outs_here, land.shape[2]), jnp.float32)
    for group_index in range(count):
        for channel in range(channels):
            row = land[group_index, channel : channel + 1, :].astype(jnp.float32)
            column = group_index * channels + channel
            total = total + w_ref[:, column : column + 1] * row
    for group_index in range(count):
        mixed[group_index] = total[group_index * outs_here : (group_index + 1) * outs_here].astype(mixed.dtype)
    trade(mixed, back, send_b, recv_b, 1)
    y_ref[...] = back[...]


def project_over_tp(x, weight, outs_here, collective):
    count, channels, block = x.shape
    return pl.pallas_call(
        _projection_kernel,
        out_shape=jax.ShapeDtypeStruct((count, outs_here, block), x.dtype),
        in_specs=[pl.BlockSpec(memory_space=pltpu.VMEM)] * 2,
        out_specs=pl.BlockSpec(memory_space=pltpu.VMEM),
        scratch_shapes=[
            pltpu.VMEM(x.shape, x.dtype),
            pltpu.VMEM((count, outs_here, block), x.dtype),
            pltpu.VMEM((count, outs_here, block), x.dtype),
            pltpu.SemaphoreType.DMA((count,)),
            pltpu.SemaphoreType.DMA((count,)),
            pltpu.SemaphoreType.DMA((count,)),
            pltpu.SemaphoreType.DMA((count,)),
            pltpu.SemaphoreType.DMA((2,)),
        ],
        compiler_params=pltpu.CompilerParams(collective_id=collective, has_side_effects=True),
    )(x, weight)


def fourier_tables(length_all):
    split = 1 << (int(math.log2(length_all)) // 2)
    rows_hi = length_all // split
    scale = 2.0 * math.pi / length_all
    columns = jnp.arange(length_all, dtype=jnp.int32)
    low = jnp.arange(split, dtype=jnp.int32)
    high = jnp.arange(rows_hi, dtype=jnp.int32)
    angle_low = (low[:, None] * columns[None, :] % length_all).astype(jnp.float32) * scale
    angle_high = (split * high[:, None] * columns[None, :] % length_all).astype(jnp.float32) * scale
    cos_low, sin_low = jnp.cos(angle_low)[None], jnp.sin(angle_low)[None]
    cos_high, sin_high = jnp.cos(angle_high)[:, None], jnp.sin(angle_high)[:, None]
    cosine = (cos_high * cos_low - sin_high * sin_low).reshape(length_all, length_all)
    sine = (sin_high * cos_low + cos_high * sin_low).reshape(length_all, length_all)
    return lax.optimization_barrier((cosine.astype(jnp.bfloat16), sine.astype(jnp.bfloat16)))


def twist_tables(left_index, right_index, length_all):
    phase_index = left_index[:, None] * right_index[None, :] % length_all
    angles = phase_index.astype(jnp.float32) * (2.0 * math.pi / length_all)
    return (jnp.cos(angles), jnp.sin(angles))


def contract(form, left, right):
    return jnp.einsum(form, left, right, preferred_element_type=jnp.float32)


def local(k_feature, v_feature, q_feature, spectrum, skip_gain, out_weight):
    channels, tokens = k_feature.shape
    block_order = spectrum.shape[3]
    length_all = block_order * block_order
    ctx_count = lax.axis_size("ctx")
    tp_count = lax.axis_size("tp")
    halves = 2
    group = ctx_count // halves
    slab = block_order // group
    freq_rows = block_order // ctx_count
    half_freqs = block_order // halves
    rows_here = tokens // block_order
    half_rows = block_order // 2
    ctx_index = lax.axis_index("ctx")
    half_index = ctx_index // group
    group_index = ctx_index - half_index * group
    product = (k_feature.astype(jnp.float32) * v_feature.astype(jnp.float32)).astype(jnp.bfloat16)
    cosine_full, sine_full = fourier_tables(block_order)
    both_full = jnp.stack([cosine_full, sine_full])
    both_sub = lax.dynamic_slice_in_dim(both_full, half_index * half_freqs, half_freqs, 1)[:, :, :half_rows]
    my_freqs = half_index * half_freqs + jnp.arange(half_freqs, dtype=jnp.int32)
    my_columns = group_index * slab + jnp.arange(slab, dtype=jnp.int32)
    local_ticks = ctx_index * freq_rows + jnp.arange(freq_rows, dtype=jnp.int32)
    positions = jnp.arange(block_order, dtype=jnp.int32)

    outgoing = product.reshape(channels, rows_here, group, slab).transpose(2, 0, 1, 3)
    arrived = exchange(outgoing.reshape(group, channels, -1), "ctx", False, 0, ctx_count)
    grid_rows = (
        arrived.reshape(ctx_count, channels, rows_here, slab)
        .transpose(1, 0, 2, 3)
        .reshape(channels, half_rows, slab)
    )
    first = contract("sai,cij->scaj", both_sub, grid_rows)
    twist_cosine, twist_sine = twist_tables(my_freqs, my_columns, length_all)
    spread = jnp.stack(
        [
            first[0] * twist_cosine - first[1] * twist_sine,
            -first[1] * twist_cosine - first[0] * twist_sine,
        ]
    ).astype(jnp.bfloat16)

    outgoing = spread.reshape(2, channels, group, freq_rows, slab).transpose(2, 0, 1, 3, 4)
    arrived = exchange(outgoing.reshape(group, -1, 128), "ctx", False, 1)
    block = (
        arrived.reshape(group, 2, channels, freq_rows, slab)
        .transpose(1, 2, 3, 0, 4)
        .reshape(2, channels, freq_rows, block_order)
    )
    freq = contract("rcaj,sjb->srcab", block, both_full)
    freq_real = freq[0, 0] + freq[1, 1]
    freq_imag = freq[0, 1] - freq[1, 0]
    resp_real = spectrum[0].astype(jnp.float32)
    resp_imag = spectrum[1].astype(jnp.float32)
    shaped = jnp.stack(
        [
            freq_real * resp_real - freq_imag * resp_imag,
            freq_real * resp_imag + freq_imag * resp_real,
        ]
    ).astype(jnp.bfloat16)
    inner = contract("rcab,sbj->srcaj", shaped, both_full)
    inner_real = inner[0, 0] - inner[1, 1]
    inner_imag = inner[0, 1] + inner[1, 0]
    twist_cosine, twist_sine = twist_tables(local_ticks, positions, length_all)
    back = jnp.stack(
        [
            inner_real * twist_cosine - inner_imag * twist_sine,
            inner_imag * twist_cosine + inner_real * twist_sine,
        ]
    ).astype(jnp.bfloat16)

    back = lax.optimization_barrier(back)
    outgoing = back.reshape(2, channels, freq_rows, group, slab).transpose(3, 0, 1, 2, 4)
    arrived = exchange(outgoing.reshape(group, -1, 128), "ctx", False, 2)
    columns = (
        arrived.reshape(group, 2, channels, freq_rows, slab)
        .transpose(1, 2, 0, 3, 4)
        .reshape(2, channels, half_freqs, slab)
    )
    parts = contract("sai,rcaj->srcij", both_sub, columns)
    partial = ((parts[0, 0] - parts[1, 1]) * (1.0 / length_all)).astype(jnp.bfloat16)

    outgoing = partial.reshape(channels, ctx_count, rows_here, slab).transpose(1, 0, 2, 3)
    arrived = exchange(outgoing.reshape(ctx_count, channels, -1), "ctx", False, 3)
    convolved = (
        arrived.reshape(halves, group, channels, rows_here, slab)
        .astype(jnp.float32)
        .sum(0)
        .transpose(1, 2, 0, 3)
        .reshape(channels, tokens)
        .astype(jnp.bfloat16)
    )
    gated_rows = (
        q_feature.astype(jnp.float32)
        * (convolved.astype(jnp.float32) + skip_gain[:, None] * product.astype(jnp.float32))
    ).astype(jnp.bfloat16)
    token_block = tokens // tp_count
    outgoing = gated_rows.reshape(channels, tp_count, token_block).transpose(1, 0, 2)
    outs_here = out_weight.shape[1] // tp_count
    weight_columns = out_weight.astype(jnp.float32).T
    returned = project_over_tp(outgoing, weight_columns, outs_here, 4)
    return returned.transpose(1, 0, 2).reshape(outs_here, tokens)


def solution(mesh):
    placed = (
        P("tp", "ctx"),
        P("tp", "ctx"),
        P("tp", "ctx"),
        P(None, "tp", "ctx", None),
        P("tp"),
        P(),
    )
    return jax.shard_map(
        local, mesh=mesh, in_specs=placed, out_specs=P("tp", "ctx"), check_vma=False
    )
```

```python
import functools
import math

import jax
import jax.numpy as jnp
from jax import lax
from jax.experimental import pallas as pl
from jax.experimental.pallas import tpu as pltpu
from jax.sharding import PartitionSpec as P

MESH = pl.DeviceIdType.MESH


def _exchange_kernel(axis, gather, x_ref, y_ref, land, send_sem, recv_sem, local_sem):
    count = land.shape[0]
    me = lax.rem(lax.axis_index(axis), count)
    base = lax.axis_index(axis) - me
    barrier = pltpu.get_barrier_semaphore()

    def greet(step, carry):
        peer = lax.rem(me + step, count)
        pl.semaphore_signal(barrier, 1, device_id={axis: base + peer}, device_id_type=MESH)
        return carry

    lax.fori_loop(1, count, greet, 0)
    pl.semaphore_wait(barrier, count - 1)

    def piece(peer):
        return x_ref if gather else x_ref.at[lax.rem(peer, x_ref.shape[0])]

    def outgoing(peer):
        return pltpu.make_async_remote_copy(
            src_ref=piece(peer), dst_ref=land.at[me], send_sem=send_sem.at[peer],
            recv_sem=recv_sem.at[me], device_id={axis: base + peer}, device_id_type=MESH)

    def incoming(source):
        return pltpu.make_async_remote_copy(
            src_ref=piece(source), dst_ref=land.at[source], send_sem=send_sem.at[source],
            recv_sem=recv_sem.at[source], device_id={axis: base + source}, device_id_type=MESH)

    def send(step, carry):
        outgoing(lax.rem(me + step, count)).start()
        return carry

    lax.fori_loop(1, count, send, 0)
    local = pltpu.make_async_copy(piece(me), land.at[me], local_sem)
    local.start()

    def finish(step, carry):
        outgoing(lax.rem(me + step, count)).wait_send()
        incoming(lax.rem(me + count - step, count)).wait_recv()
        return carry

    lax.fori_loop(1, count, finish, 0)
    local.wait()
    y_ref[...] = land[...]


def exchange(x, axis, gather, collective, count=None):
    count = count or (lax.axis_size(axis) if gather else x.shape[0])
    chunk = x.shape if gather else x.shape[1:]
    full = (count,) + tuple(chunk)
    return pl.pallas_call(
        functools.partial(_exchange_kernel, axis, gather),
        out_shape=jax.ShapeDtypeStruct(full, x.dtype),
        in_specs=[pl.BlockSpec(memory_space=pltpu.VMEM)],
        out_specs=pl.BlockSpec(memory_space=pltpu.VMEM),
        scratch_shapes=[
            pltpu.VMEM(full, x.dtype),
            pltpu.SemaphoreType.DMA((count,)),
            pltpu.SemaphoreType.DMA((count,)),
            pltpu.SemaphoreType.DMA,
        ],
        compiler_params=pltpu.CompilerParams(collective_id=collective, has_side_effects=True),
    )(x)


def _projection_kernel(x_ref, w_ref, y_ref, land, mixed, back, send_a, recv_a, send_b, recv_b, own):
    count, channels = land.shape[0], land.shape[1]
    outs_here = mixed.shape[1]
    me = lax.axis_index("tp")
    barrier = pltpu.get_barrier_semaphore()

    def greet(step, carry):
        pl.semaphore_signal(barrier, 1, device_id={"tp": lax.rem(me + step, count)}, device_id_type=MESH)
        return carry

    lax.fori_loop(1, count, greet, 0)
    pl.semaphore_wait(barrier, count - 1)

    def there(src, dst, sends, recvs, peer, slot):
        return pltpu.make_async_remote_copy(
            src_ref=src.at[peer], dst_ref=dst.at[slot], send_sem=sends.at[peer],
            recv_sem=recvs.at[slot], device_id={"tp": peer}, device_id_type=MESH)

    def trade(src, dst, sends, recvs, flag):
        def send(step, carry):
            there(src, dst, sends, recvs, lax.rem(me + step, count), me).start()
            return carry

        lax.fori_loop(1, count, send, 0)
        local = pltpu.make_async_copy(src.at[me], dst.at[me], own.at[flag])
        local.start()

        def finish(step, carry):
            there(src, dst, sends, recvs, lax.rem(me + step, count), me).wait_send()
            source = lax.rem(me + count - step, count)
            there(src, dst, sends, recvs, source, source).wait_recv()
            return carry

        lax.fori_loop(1, count, finish, 0)
        local.wait()

    trade(x_ref, land, send_a, recv_a, 0)
    total = jnp.zeros((count * outs_here, land.shape[2]), jnp.float32)
    for group_index in range(count):
        for channel in range(channels):
            row = land[group_index, channel : channel + 1, :].astype(jnp.float32)
            column = group_index * channels + channel
            total = total + w_ref[:, column : column + 1] * row
    for group_index in range(count):
        mixed[group_index] = total[group_index * outs_here : (group_index + 1) * outs_here].astype(mixed.dtype)
    trade(mixed, back, send_b, recv_b, 1)
    block = land.shape[2]
    for group_index in range(count):
        y_ref[:, group_index * block : (group_index + 1) * block] = back[group_index]


def project_over_tp(x, weight, outs_here, collective):
    count, channels, block = x.shape
    return pl.pallas_call(
        _projection_kernel,
        out_shape=jax.ShapeDtypeStruct((outs_here, count * block), x.dtype),
        in_specs=[pl.BlockSpec(memory_space=pltpu.VMEM)] * 2,
        out_specs=pl.BlockSpec(memory_space=pltpu.VMEM),
        scratch_shapes=[
            pltpu.VMEM(x.shape, x.dtype),
            pltpu.VMEM((count, outs_here, block), x.dtype),
            pltpu.VMEM((count, outs_here, block), x.dtype),
            pltpu.SemaphoreType.DMA((count,)),
            pltpu.SemaphoreType.DMA((count,)),
            pltpu.SemaphoreType.DMA((count,)),
            pltpu.SemaphoreType.DMA((count,)),
            pltpu.SemaphoreType.DMA((2,)),
        ],
        compiler_params=pltpu.CompilerParams(collective_id=collective, has_side_effects=True),
    )(x, weight)


def fourier_tables(length_all):
    split = 1 << (int(math.log2(length_all)) // 2)
    rows_hi = length_all // split
    scale = 2.0 * math.pi / length_all
    columns = jnp.arange(length_all, dtype=jnp.int32)
    low = jnp.arange(split, dtype=jnp.int32)
    high = jnp.arange(rows_hi, dtype=jnp.int32)
    angle_low = (low[:, None] * columns[None, :] % length_all).astype(jnp.float32) * scale
    angle_high = (split * high[:, None] * columns[None, :] % length_all).astype(jnp.float32) * scale
    cos_low, sin_low = jnp.cos(angle_low)[None], jnp.sin(angle_low)[None]
    cos_high, sin_high = jnp.cos(angle_high)[:, None], jnp.sin(angle_high)[:, None]
    cosine = (cos_high * cos_low - sin_high * sin_low).reshape(length_all, length_all)
    sine = (sin_high * cos_low + cos_high * sin_low).reshape(length_all, length_all)
    return lax.optimization_barrier((cosine.astype(jnp.bfloat16), sine.astype(jnp.bfloat16)))


def twist_tables(left_index, right_index, length_all):
    phase_index = left_index[:, None] * right_index[None, :] % length_all
    angles = phase_index.astype(jnp.float32) * (2.0 * math.pi / length_all)
    return (jnp.cos(angles), jnp.sin(angles))


def contract(form, left, right):
    return jnp.einsum(form, left, right, preferred_element_type=jnp.float32)


def local(k_feature, v_feature, q_feature, spectrum, skip_gain, out_weight):
    channels, tokens = k_feature.shape
    block_order = spectrum.shape[3]
    length_all = block_order * block_order
    ctx_count = lax.axis_size("ctx")
    tp_count = lax.axis_size("tp")
    halves = 2
    group = ctx_count // halves
    slab = block_order // group
    freq_rows = block_order // ctx_count
    half_freqs = block_order // halves
    rows_here = tokens // block_order
    half_rows = block_order // 2
    ctx_index = lax.axis_index("ctx")
    half_index = ctx_index // group
    group_index = ctx_index - half_index * group
    product = (k_feature.astype(jnp.float32) * v_feature.astype(jnp.float32)).astype(jnp.bfloat16)
    cosine_full, sine_full = fourier_tables(block_order)
    both_full = jnp.stack([cosine_full, sine_full])
    both_sub = lax.dynamic_slice_in_dim(both_full, half_index * half_freqs, half_freqs, 1)[:, :, :half_rows]
    my_freqs = half_index * half_freqs + jnp.arange(half_freqs, dtype=jnp.int32)
    my_columns = group_index * slab + jnp.arange(slab, dtype=jnp.int32)
    local_ticks = ctx_index * freq_rows + jnp.arange(freq_rows, dtype=jnp.int32)
    positions = jnp.arange(block_order, dtype=jnp.int32)

    outgoing = product.reshape(channels, rows_here, group, slab).transpose(2, 0, 1, 3)
    arrived = exchange(outgoing.reshape(group, channels, -1), "ctx", False, 0, ctx_count)
    grid_rows = (
        arrived.reshape(ctx_count, channels, rows_here, slab)
        .transpose(1, 0, 2, 3)
        .reshape(channels, half_rows, slab)
    )
    first = contract("sai,cij->scaj", both_sub, grid_rows)
    twist_cosine, twist_sine = twist_tables(my_freqs, my_columns, length_all)
    spread = jnp.stack(
        [
            first[0] * twist_cosine - first[1] * twist_sine,
            -first[1] * twist_cosine - first[0] * twist_sine,
        ]
    ).astype(jnp.bfloat16)

    outgoing = spread.reshape(2, channels, group, freq_rows, slab).transpose(2, 0, 1, 3, 4)
    arrived = exchange(outgoing.reshape(group, -1, 128), "ctx", False, 1)
    block = (
        arrived.reshape(group, 2, channels, freq_rows, slab)
        .transpose(1, 2, 3, 0, 4)
        .reshape(2, channels, freq_rows, block_order)
    )
    freq = contract("rcaj,sjb->srcab", block, both_full)
    freq_real = freq[0, 0] + freq[1, 1]
    freq_imag = freq[0, 1] - freq[1, 0]
    resp_real = spectrum[0].astype(jnp.float32)
    resp_imag = spectrum[1].astype(jnp.float32)
    shaped = jnp.stack(
        [
            freq_real * resp_real - freq_imag * resp_imag,
            freq_real * resp_imag + freq_imag * resp_real,
        ]
    ).astype(jnp.bfloat16)
    inner = contract("rcab,sbj->srcaj", shaped, both_full)
    inner_real = inner[0, 0] - inner[1, 1]
    inner_imag = inner[0, 1] + inner[1, 0]
    twist_cosine, twist_sine = twist_tables(local_ticks, positions, length_all)
    back = jnp.stack(
        [
            inner_real * twist_cosine - inner_imag * twist_sine,
            inner_imag * twist_cosine + inner_real * twist_sine,
        ]
    ).astype(jnp.bfloat16)

    back = lax.optimization_barrier(back)
    outgoing = back.reshape(2, channels, freq_rows, group, slab).transpose(3, 0, 1, 2, 4)
    arrived = exchange(outgoing.reshape(group, -1, 128), "ctx", False, 2)
    columns = (
        arrived.reshape(group, 2, channels, freq_rows, slab)
        .transpose(1, 2, 0, 3, 4)
        .reshape(2, channels, half_freqs, slab)
    )
    parts = contract("sai,rcaj->srcij", both_sub, columns)
    partial = ((parts[0, 0] - parts[1, 1]) * (1.0 / length_all)).astype(jnp.bfloat16)

    outgoing = partial.reshape(channels, ctx_count, rows_here, slab).transpose(1, 0, 2, 3)
    arrived = exchange(outgoing.reshape(ctx_count, channels, -1), "ctx", False, 3)
    convolved = (
        arrived.reshape(halves, group, channels, rows_here, slab)
        .astype(jnp.float32)
        .sum(0)
        .transpose(1, 2, 0, 3)
        .reshape(channels, tokens)
        .astype(jnp.bfloat16)
    )
    gated_rows = (
        q_feature.astype(jnp.float32)
        * (convolved.astype(jnp.float32) + skip_gain[:, None] * product.astype(jnp.float32))
    ).astype(jnp.bfloat16)
    token_block = tokens // tp_count
    outgoing = gated_rows.reshape(channels, tp_count, token_block).transpose(1, 0, 2)
    outs_here = out_weight.shape[1] // tp_count
    weight_columns = out_weight.astype(jnp.float32).T
    return project_over_tp(outgoing, weight_columns, outs_here, 4)


def solution(mesh):
    placed = (
        P("tp", "ctx"),
        P("tp", "ctx"),
        P("tp", "ctx"),
        P(None, "tp", "ctx", None),
        P("tp"),
        P(),
    )
    return jax.shard_map(
        local, mesh=mesh, in_specs=placed, out_specs=P("tp", "ctx"), check_vma=False
    )
```

```python
import functools
import math

import jax
import jax.numpy as jnp
from jax import lax
from jax.experimental import pallas as pl
from jax.experimental.pallas import tpu as pltpu
from jax.sharding import PartitionSpec as P

MESH = pl.DeviceIdType.MESH


def _exchange_kernel(axis, gather, x_ref, y_ref, land, send_sem, recv_sem, local_sem):
    count = land.shape[0]
    me = lax.rem(lax.axis_index(axis), count)
    base = lax.axis_index(axis) - me
    barrier = pltpu.get_barrier_semaphore()

    def greet(step, carry):
        peer = lax.rem(me + step, count)
        pl.semaphore_signal(barrier, 1, device_id={axis: base + peer}, device_id_type=MESH)
        return carry

    lax.fori_loop(1, count, greet, 0)
    pl.semaphore_wait(barrier, count - 1)

    def piece(peer):
        return x_ref if gather else x_ref.at[lax.rem(peer, x_ref.shape[0])]

    def outgoing(peer):
        return pltpu.make_async_remote_copy(
            src_ref=piece(peer), dst_ref=land.at[me], send_sem=send_sem.at[peer],
            recv_sem=recv_sem.at[me], device_id={axis: base + peer}, device_id_type=MESH)

    def incoming(source):
        return pltpu.make_async_remote_copy(
            src_ref=piece(source), dst_ref=land.at[source], send_sem=send_sem.at[source],
            recv_sem=recv_sem.at[source], device_id={axis: base + source}, device_id_type=MESH)

    def send(step, carry):
        outgoing(lax.rem(me + step, count)).start()
        return carry

    lax.fori_loop(1, count, send, 0)
    local = pltpu.make_async_copy(piece(me), land.at[me], local_sem)
    local.start()

    def finish(step, carry):
        outgoing(lax.rem(me + step, count)).wait_send()
        incoming(lax.rem(me + count - step, count)).wait_recv()
        return carry

    lax.fori_loop(1, count, finish, 0)
    local.wait()
    y_ref[...] = land[...]


def exchange(x, axis, gather, collective, count=None):
    count = count or (lax.axis_size(axis) if gather else x.shape[0])
    chunk = x.shape if gather else x.shape[1:]
    full = (count,) + tuple(chunk)
    return pl.pallas_call(
        functools.partial(_exchange_kernel, axis, gather),
        out_shape=jax.ShapeDtypeStruct(full, x.dtype),
        in_specs=[pl.BlockSpec(memory_space=pltpu.VMEM)],
        out_specs=pl.BlockSpec(memory_space=pltpu.VMEM),
        scratch_shapes=[
            pltpu.VMEM(full, x.dtype),
            pltpu.SemaphoreType.DMA((count,)),
            pltpu.SemaphoreType.DMA((count,)),
            pltpu.SemaphoreType.DMA,
        ],
        compiler_params=pltpu.CompilerParams(collective_id=collective, has_side_effects=True),
    )(x)


def _projection_kernel(x_ref, w_ref, y_ref, land, mixed, back, send_a, recv_a, send_b, recv_b, own):
    count, channels = land.shape[0], land.shape[1]
    outs_here = mixed.shape[1]
    me = lax.axis_index("tp")
    barrier = pltpu.get_barrier_semaphore()

    def greet(step, carry):
        pl.semaphore_signal(barrier, 1, device_id={"tp": lax.rem(me + step, count)}, device_id_type=MESH)
        return carry

    lax.fori_loop(1, count, greet, 0)
    pl.semaphore_wait(barrier, count - 1)

    def there(src, dst, sends, recvs, peer, slot):
        return pltpu.make_async_remote_copy(
            src_ref=src.at[peer], dst_ref=dst.at[slot], send_sem=sends.at[peer],
            recv_sem=recvs.at[slot], device_id={"tp": peer}, device_id_type=MESH)

    def trade(src, dst, sends, recvs, flag):
        def send(step, carry):
            there(src, dst, sends, recvs, lax.rem(me + step, count), me).start()
            return carry

        lax.fori_loop(1, count, send, 0)
        local = pltpu.make_async_copy(src.at[me], dst.at[me], own.at[flag])
        local.start()

        def finish(step, carry):
            there(src, dst, sends, recvs, lax.rem(me + step, count), me).wait_send()
            source = lax.rem(me + count - step, count)
            there(src, dst, sends, recvs, source, source).wait_recv()
            return carry

        lax.fori_loop(1, count, finish, 0)
        local.wait()

    trade(x_ref, land, send_a, recv_a, 0)
    total = jnp.dot(
        w_ref[...], land[...].reshape(count * channels, land.shape[2]), preferred_element_type=jnp.float32
    )
    for group_index in range(count):
        mixed[group_index] = total[group_index * outs_here : (group_index + 1) * outs_here].astype(mixed.dtype)
    trade(mixed, back, send_b, recv_b, 1)
    block = land.shape[2]
    for group_index in range(count):
        y_ref[:, group_index * block : (group_index + 1) * block] = back[group_index]


def project_over_tp(x, weight, outs_here, collective):
    count, channels, block = x.shape
    return pl.pallas_call(
        _projection_kernel,
        out_shape=jax.ShapeDtypeStruct((outs_here, count * block), x.dtype),
        in_specs=[pl.BlockSpec(memory_space=pltpu.VMEM)] * 2,
        out_specs=pl.BlockSpec(memory_space=pltpu.VMEM),
        scratch_shapes=[
            pltpu.VMEM(x.shape, x.dtype),
            pltpu.VMEM((count, outs_here, block), x.dtype),
            pltpu.VMEM((count, outs_here, block), x.dtype),
            pltpu.SemaphoreType.DMA((count,)),
            pltpu.SemaphoreType.DMA((count,)),
            pltpu.SemaphoreType.DMA((count,)),
            pltpu.SemaphoreType.DMA((count,)),
            pltpu.SemaphoreType.DMA((2,)),
        ],
        compiler_params=pltpu.CompilerParams(collective_id=collective, has_side_effects=True),
    )(x, weight)


def fourier_tables(length_all):
    split = 1 << (int(math.log2(length_all)) // 2)
    rows_hi = length_all // split
    scale = 2.0 * math.pi / length_all
    columns = jnp.arange(length_all, dtype=jnp.int32)
    low = jnp.arange(split, dtype=jnp.int32)
    high = jnp.arange(rows_hi, dtype=jnp.int32)
    angle_low = (low[:, None] * columns[None, :] % length_all).astype(jnp.float32) * scale
    angle_high = (split * high[:, None] * columns[None, :] % length_all).astype(jnp.float32) * scale
    cos_low, sin_low = jnp.cos(angle_low)[None], jnp.sin(angle_low)[None]
    cos_high, sin_high = jnp.cos(angle_high)[:, None], jnp.sin(angle_high)[:, None]
    cosine = (cos_high * cos_low - sin_high * sin_low).reshape(length_all, length_all)
    sine = (sin_high * cos_low + cos_high * sin_low).reshape(length_all, length_all)
    return lax.optimization_barrier((cosine.astype(jnp.bfloat16), sine.astype(jnp.bfloat16)))


def twist_tables(left_index, right_index, length_all):
    phase_index = left_index[:, None] * right_index[None, :] % length_all
    angles = phase_index.astype(jnp.float32) * (2.0 * math.pi / length_all)
    return (jnp.cos(angles), jnp.sin(angles))


def contract(form, left, right):
    return jnp.einsum(form, left, right, preferred_element_type=jnp.float32)


def local(k_feature, v_feature, q_feature, spectrum, skip_gain, out_weight):
    channels, tokens = k_feature.shape
    block_order = spectrum.shape[3]
    length_all = block_order * block_order
    ctx_count = lax.axis_size("ctx")
    tp_count = lax.axis_size("tp")
    halves = 2
    group = ctx_count // halves
    slab = block_order // group
    freq_rows = block_order // ctx_count
    half_freqs = block_order // halves
    rows_here = tokens // block_order
    half_rows = block_order // 2
    ctx_index = lax.axis_index("ctx")
    half_index = ctx_index // group
    group_index = ctx_index - half_index * group
    product = (k_feature.astype(jnp.float32) * v_feature.astype(jnp.float32)).astype(jnp.bfloat16)
    cosine_full, sine_full = fourier_tables(block_order)
    both_full = jnp.stack([cosine_full, sine_full])
    both_sub = lax.dynamic_slice_in_dim(both_full, half_index * half_freqs, half_freqs, 1)[:, :, :half_rows]
    my_freqs = half_index * half_freqs + jnp.arange(half_freqs, dtype=jnp.int32)
    my_columns = group_index * slab + jnp.arange(slab, dtype=jnp.int32)
    local_ticks = ctx_index * freq_rows + jnp.arange(freq_rows, dtype=jnp.int32)
    positions = jnp.arange(block_order, dtype=jnp.int32)

    outgoing = product.reshape(channels, rows_here, group, slab).transpose(2, 0, 1, 3)
    arrived = exchange(outgoing.reshape(group, channels, -1), "ctx", False, 0, ctx_count)
    grid_rows = (
        arrived.reshape(ctx_count, channels, rows_here, slab)
        .transpose(1, 0, 2, 3)
        .reshape(channels, half_rows, slab)
    )
    first = contract("sai,cij->scaj", both_sub, grid_rows)
    twist_cosine, twist_sine = twist_tables(my_freqs, my_columns, length_all)
    spread = jnp.stack(
        [
            first[0] * twist_cosine - first[1] * twist_sine,
            -first[1] * twist_cosine - first[0] * twist_sine,
        ]
    ).astype(jnp.bfloat16)

    outgoing = spread.reshape(2, channels, group, freq_rows, slab).transpose(2, 0, 1, 3, 4)
    arrived = exchange(outgoing.reshape(group, -1, 128), "ctx", False, 1)
    block = (
        arrived.reshape(group, 2, channels, freq_rows, slab)
        .transpose(1, 2, 3, 0, 4)
        .reshape(2, channels, freq_rows, block_order)
    )
    freq = contract("rcaj,sjb->srcab", block, both_full)
    freq_real = freq[0, 0] + freq[1, 1]
    freq_imag = freq[0, 1] - freq[1, 0]
    resp_real = spectrum[0].astype(jnp.float32)
    resp_imag = spectrum[1].astype(jnp.float32)
    shaped = jnp.stack(
        [
            freq_real * resp_real - freq_imag * resp_imag,
            freq_real * resp_imag + freq_imag * resp_real,
        ]
    ).astype(jnp.bfloat16)
    inner = contract("rcab,sbj->srcaj", shaped, both_full)
    inner_real = inner[0, 0] - inner[1, 1]
    inner_imag = inner[0, 1] + inner[1, 0]
    twist_cosine, twist_sine = twist_tables(local_ticks, positions, length_all)
    back = jnp.stack(
        [
            inner_real * twist_cosine - inner_imag * twist_sine,
            inner_imag * twist_cosine + inner_real * twist_sine,
        ]
    ).astype(jnp.bfloat16)

    back = lax.optimization_barrier(back)
    outgoing = back.reshape(2, channels, freq_rows, group, slab).transpose(3, 0, 1, 2, 4)
    arrived = exchange(outgoing.reshape(group, -1, 128), "ctx", False, 2)
    columns = (
        arrived.reshape(group, 2, channels, freq_rows, slab)
        .transpose(1, 2, 0, 3, 4)
        .reshape(2, channels, half_freqs, slab)
    )
    parts = contract("sai,rcaj->srcij", both_sub, columns)
    partial = ((parts[0, 0] - parts[1, 1]) * (1.0 / length_all)).astype(jnp.bfloat16)

    outgoing = partial.reshape(channels, ctx_count, rows_here, slab).transpose(1, 0, 2, 3)
    arrived = exchange(outgoing.reshape(ctx_count, channels, -1), "ctx", False, 3)
    convolved = (
        arrived.reshape(halves, group, channels, rows_here, slab)
        .astype(jnp.float32)
        .sum(0)
        .transpose(1, 2, 0, 3)
        .reshape(channels, tokens)
        .astype(jnp.bfloat16)
    )
    gated_rows = (
        q_feature.astype(jnp.float32)
        * (convolved.astype(jnp.float32) + skip_gain[:, None] * product.astype(jnp.float32))
    ).astype(jnp.bfloat16)
    token_block = tokens // tp_count
    outgoing = gated_rows.reshape(channels, tp_count, token_block).transpose(1, 0, 2)
    outs_here = out_weight.shape[1] // tp_count
    weight_columns = out_weight.T
    return project_over_tp(outgoing, weight_columns, outs_here, 4)


def solution(mesh):
    placed = (
        P("tp", "ctx"),
        P("tp", "ctx"),
        P("tp", "ctx"),
        P(None, "tp", "ctx", None),
        P("tp"),
        P(),
    )
    return jax.shard_map(
        local, mesh=mesh, in_specs=placed, out_specs=P("tp", "ctx"), check_vma=False
    )
```

```python
import functools
import math

import jax
import jax.numpy as jnp
from jax import lax
from jax.experimental import pallas as pl
from jax.experimental.pallas import tpu as pltpu
from jax.sharding import PartitionSpec as P

MESH = pl.DeviceIdType.MESH


def _exchange_kernel(axis, gather, x_ref, y_ref, land, send_sem, recv_sem, local_sem):
    count = land.shape[0]
    me = lax.rem(lax.axis_index(axis), count)
    base = lax.axis_index(axis) - me
    barrier = pltpu.get_barrier_semaphore()

    def greet(step, carry):
        peer = lax.rem(me + step, count)
        pl.semaphore_signal(barrier, 1, device_id={axis: base + peer}, device_id_type=MESH)
        return carry

    def piece(peer):
        return x_ref if gather else x_ref.at[lax.rem(peer, x_ref.shape[0])]

    local = pltpu.make_async_copy(piece(me), land.at[me], local_sem)
    local.start()
    lax.fori_loop(1, count, greet, 0)
    pl.semaphore_wait(barrier, count - 1)

    def outgoing(peer):
        return pltpu.make_async_remote_copy(
            src_ref=piece(peer), dst_ref=land.at[me], send_sem=send_sem.at[peer],
            recv_sem=recv_sem.at[me], device_id={axis: base + peer}, device_id_type=MESH)

    def incoming(source):
        return pltpu.make_async_remote_copy(
            src_ref=piece(source), dst_ref=land.at[source], send_sem=send_sem.at[source],
            recv_sem=recv_sem.at[source], device_id={axis: base + source}, device_id_type=MESH)

    def send(step, carry):
        outgoing(lax.rem(me + step, count)).start()
        return carry

    lax.fori_loop(1, count, send, 0)

    def finish(step, carry):
        outgoing(lax.rem(me + step, count)).wait_send()
        incoming(lax.rem(me + count - step, count)).wait_recv()
        return carry

    lax.fori_loop(1, count, finish, 0)
    local.wait()
    y_ref[...] = land[...]


def exchange(x, axis, gather, collective, count=None):
    count = count or (lax.axis_size(axis) if gather else x.shape[0])
    chunk = x.shape if gather else x.shape[1:]
    full = (count,) + tuple(chunk)
    return pl.pallas_call(
        functools.partial(_exchange_kernel, axis, gather),
        out_shape=jax.ShapeDtypeStruct(full, x.dtype),
        in_specs=[pl.BlockSpec(memory_space=pltpu.VMEM)],
        out_specs=pl.BlockSpec(memory_space=pltpu.VMEM),
        scratch_shapes=[
            pltpu.VMEM(full, x.dtype),
            pltpu.SemaphoreType.DMA((count,)),
            pltpu.SemaphoreType.DMA((count,)),
            pltpu.SemaphoreType.DMA,
        ],
        compiler_params=pltpu.CompilerParams(collective_id=collective, has_side_effects=True),
    )(x)


def _projection_kernel(x_ref, w_ref, y_ref, land, mixed, back, send_a, recv_a, send_b, recv_b, own):
    count, channels = land.shape[0], land.shape[1]
    outs_here = mixed.shape[1]
    me = lax.axis_index("tp")
    barrier = pltpu.get_barrier_semaphore()

    def greet(step, carry):
        pl.semaphore_signal(barrier, 1, device_id={"tp": lax.rem(me + step, count)}, device_id_type=MESH)
        return carry

    lax.fori_loop(1, count, greet, 0)
    pl.semaphore_wait(barrier, count - 1)

    def there(src, dst, sends, recvs, peer, slot):
        return pltpu.make_async_remote_copy(
            src_ref=src.at[peer], dst_ref=dst.at[slot], send_sem=sends.at[peer],
            recv_sem=recvs.at[slot], device_id={"tp": peer}, device_id_type=MESH)

    def trade(src, dst, sends, recvs, flag):
        def send(step, carry):
            there(src, dst, sends, recvs, lax.rem(me + step, count), me).start()
            return carry

        lax.fori_loop(1, count, send, 0)
        local = pltpu.make_async_copy(src.at[me], dst.at[me], own.at[flag])
        local.start()

        def finish(step, carry):
            there(src, dst, sends, recvs, lax.rem(me + step, count), me).wait_send()
            source = lax.rem(me + count - step, count)
            there(src, dst, sends, recvs, source, source).wait_recv()
            return carry

        lax.fori_loop(1, count, finish, 0)
        local.wait()

    trade(x_ref, land, send_a, recv_a, 0)
    total = jnp.dot(
        w_ref[...], land[...].reshape(count * channels, land.shape[2]), preferred_element_type=jnp.float32
    )
    for group_index in range(count):
        mixed[group_index] = total[group_index * outs_here : (group_index + 1) * outs_here].astype(mixed.dtype)
    trade(mixed, back, send_b, recv_b, 1)
    block = land.shape[2]
    for group_index in range(count):
        y_ref[:, group_index * block : (group_index + 1) * block] = back[group_index]


def project_over_tp(x, weight, outs_here, collective):
    count, channels, block = x.shape
    return pl.pallas_call(
        _projection_kernel,
        out_shape=jax.ShapeDtypeStruct((outs_here, count * block), x.dtype),
        in_specs=[pl.BlockSpec(memory_space=pltpu.VMEM)] * 2,
        out_specs=pl.BlockSpec(memory_space=pltpu.VMEM),
        scratch_shapes=[
            pltpu.VMEM(x.shape, x.dtype),
            pltpu.VMEM((count, outs_here, block), x.dtype),
            pltpu.VMEM((count, outs_here, block), x.dtype),
            pltpu.SemaphoreType.DMA((count,)),
            pltpu.SemaphoreType.DMA((count,)),
            pltpu.SemaphoreType.DMA((count,)),
            pltpu.SemaphoreType.DMA((count,)),
            pltpu.SemaphoreType.DMA((2,)),
        ],
        compiler_params=pltpu.CompilerParams(collective_id=collective, has_side_effects=True),
    )(x, weight)


def fourier_tables(length_all):
    split = 1 << (int(math.log2(length_all)) // 2)
    rows_hi = length_all // split
    scale = 2.0 * math.pi / length_all
    columns = jnp.arange(length_all, dtype=jnp.int32)
    low = jnp.arange(split, dtype=jnp.int32)
    high = jnp.arange(rows_hi, dtype=jnp.int32)
    angle_low = (low[:, None] * columns[None, :] % length_all).astype(jnp.float32) * scale
    angle_high = (split * high[:, None] * columns[None, :] % length_all).astype(jnp.float32) * scale
    cos_low, sin_low = jnp.cos(angle_low)[None], jnp.sin(angle_low)[None]
    cos_high, sin_high = jnp.cos(angle_high)[:, None], jnp.sin(angle_high)[:, None]
    cosine = (cos_high * cos_low - sin_high * sin_low).reshape(length_all, length_all)
    sine = (sin_high * cos_low + cos_high * sin_low).reshape(length_all, length_all)
    return lax.optimization_barrier((cosine.astype(jnp.bfloat16), sine.astype(jnp.bfloat16)))


def twist_tables(left_index, right_index, length_all):
    phase_index = left_index[:, None] * right_index[None, :] % length_all
    angles = phase_index.astype(jnp.float32) * (2.0 * math.pi / length_all)
    return (jnp.cos(angles), jnp.sin(angles))


def contract(form, left, right):
    return jnp.einsum(form, left, right, preferred_element_type=jnp.float32)


def local(k_feature, v_feature, q_feature, spectrum, skip_gain, out_weight):
    channels, tokens = k_feature.shape
    block_order = spectrum.shape[3]
    length_all = block_order * block_order
    ctx_count = lax.axis_size("ctx")
    tp_count = lax.axis_size("tp")
    halves = 2
    group = ctx_count // halves
    slab = block_order // group
    freq_rows = block_order // ctx_count
    half_freqs = block_order // halves
    rows_here = tokens // block_order
    half_rows = block_order // 2
    ctx_index = lax.axis_index("ctx")
    half_index = ctx_index // group
    group_index = ctx_index - half_index * group
    product = (k_feature.astype(jnp.float32) * v_feature.astype(jnp.float32)).astype(jnp.bfloat16)
    cosine_full, sine_full = fourier_tables(block_order)
    both_full = jnp.stack([cosine_full, sine_full])
    both_sub = lax.dynamic_slice_in_dim(both_full, half_index * half_freqs, half_freqs, 1)[:, :, :half_rows]
    my_freqs = half_index * half_freqs + jnp.arange(half_freqs, dtype=jnp.int32)
    my_columns = group_index * slab + jnp.arange(slab, dtype=jnp.int32)
    local_ticks = ctx_index * freq_rows + jnp.arange(freq_rows, dtype=jnp.int32)
    positions = jnp.arange(block_order, dtype=jnp.int32)

    outgoing = product.reshape(channels, rows_here, group, slab).transpose(2, 0, 1, 3)
    arrived = exchange(outgoing.reshape(group, channels, -1), "ctx", False, 0, ctx_count)
    grid_rows = (
        arrived.reshape(ctx_count, channels, rows_here, slab)
        .transpose(1, 0, 2, 3)
        .reshape(channels, half_rows, slab)
    )
    first = contract("sai,cij->scaj", both_sub, grid_rows)
    twist_cosine, twist_sine = twist_tables(my_freqs, my_columns, length_all)
    spread = jnp.stack(
        [
            first[0] * twist_cosine - first[1] * twist_sine,
            -first[1] * twist_cosine - first[0] * twist_sine,
        ]
    ).astype(jnp.bfloat16)

    outgoing = spread.reshape(2, channels, group, freq_rows, slab).transpose(2, 0, 1, 3, 4)
    arrived = exchange(outgoing.reshape(group, -1, 128), "ctx", False, 1)
    block = (
        arrived.reshape(group, 2, channels, freq_rows, slab)
        .transpose(1, 2, 3, 0, 4)
        .reshape(2, channels, freq_rows, block_order)
    )
    freq = contract("rcaj,sjb->srcab", block, both_full)
    freq_real = freq[0, 0] + freq[1, 1]
    freq_imag = freq[0, 1] - freq[1, 0]
    resp_real = spectrum[0].astype(jnp.float32)
    resp_imag = spectrum[1].astype(jnp.float32)
    shaped = jnp.stack(
        [
            freq_real * resp_real - freq_imag * resp_imag,
            freq_real * resp_imag + freq_imag * resp_real,
        ]
    ).astype(jnp.bfloat16)
    inner = contract("rcab,sbj->srcaj", shaped, both_full)
    inner_real = inner[0, 0] - inner[1, 1]
    inner_imag = inner[0, 1] + inner[1, 0]
    twist_cosine, twist_sine = twist_tables(local_ticks, positions, length_all)
    back = jnp.stack(
        [
            inner_real * twist_cosine - inner_imag * twist_sine,
            inner_imag * twist_cosine + inner_real * twist_sine,
        ]
    ).astype(jnp.bfloat16)

    back = lax.optimization_barrier(back)
    outgoing = back.reshape(2, channels, freq_rows, group, slab).transpose(3, 0, 1, 2, 4)
    arrived = exchange(outgoing.reshape(group, -1, 128), "ctx", False, 2)
    columns = (
        arrived.reshape(group, 2, channels, freq_rows, slab)
        .transpose(1, 2, 0, 3, 4)
        .reshape(2, channels, half_freqs, slab)
    )
    parts = contract("sai,rcaj->srcij", both_sub, columns)
    partial = ((parts[0, 0] - parts[1, 1]) * (1.0 / length_all)).astype(jnp.bfloat16)

    outgoing = partial.reshape(channels, ctx_count, rows_here, slab).transpose(1, 0, 2, 3)
    arrived = exchange(outgoing.reshape(ctx_count, channels, -1), "ctx", False, 3)
    convolved = (
        arrived.reshape(halves, group, channels, rows_here, slab)
        .astype(jnp.float32)
        .sum(0)
        .transpose(1, 2, 0, 3)
        .reshape(channels, tokens)
        .astype(jnp.bfloat16)
    )
    gated_rows = (
        q_feature.astype(jnp.float32)
        * (convolved.astype(jnp.float32) + skip_gain[:, None] * product.astype(jnp.float32))
    ).astype(jnp.bfloat16)
    token_block = tokens // tp_count
    outgoing = gated_rows.reshape(channels, tp_count, token_block).transpose(1, 0, 2)
    outs_here = out_weight.shape[1] // tp_count
    weight_columns = out_weight.T
    return project_over_tp(outgoing, weight_columns, outs_here, 4)


def solution(mesh):
    placed = (
        P("tp", "ctx"),
        P("tp", "ctx"),
        P("tp", "ctx"),
        P(None, "tp", "ctx", None),
        P("tp"),
        P(),
    )
    return jax.shard_map(
        local, mesh=mesh, in_specs=placed, out_specs=P("tp", "ctx"), check_vma=False
    )
```
